512 devices in a mesh: expert: 32 (over z, core), dp: 4 (over x), tensor: 4 (over y).
Axes of the slice: x: 4, y: 4, z: 16, core: 2. Of those that a mesh axis runs over, the one named last changes fastest.
Arguments:
- tokens: bfloat16 [2, 4096, 7168], P(None, ('expert', 'dp')), may hold values from -6 to 6
- cotangent: bfloat16 [2, 4096, 7168], P(None, ('expert', 'dp')), may hold values from -0.625 to 0.625
- route_gate: bfloat16 [2, 4096, 2], P(None, ('expert', 'dp')), may hold values from 0.19921875 to 1
- routes: int32 [2, 4096, 2], P(None, ('expert', 'dp')), may hold values from 0 to 31, all different within a row; in each aligned block of 32 rows (0 to 31, 32 to 63, ..., all dimensions but the last counted through in order) at most 3 rows name the same one
- gate_weight: bfloat16 [32, 7168, 1024], P('expert', 'dp', 'tensor'), may hold values from -0.0625 to 0.0625
- up_weight: bfloat16 [32, 7168, 1024], P('expert', 'dp', 'tensor'), may hold values from -0.0625 to 0.0625
- down_weight: bfloat16 [32, 1024, 7168], P('expert', 'tensor', 'dp'), may hold values from -0.1875 to 0.1875
- dropped: int32 [32, 3], P('expert'), may hold values from 0 to 7, as said below
Outputs:
- saliency: float32 [2, 32, 1024], P(None, 'expert', 'tensor')
- compact_down: bfloat16 [32, 640, 7168], P('expert', 'tensor', 'dp')
The draws below stay inside these ranges and needn't reach their ends.
Inputs may be any that keep to these rules, and one draw needn't show every extreme that they name: `routes`: each token names 2 different experts. Among the 32 tokens of one set on one index of expert and dp, no expert is named more than 3 times, a bound that some block reaches. `dropped`: each row lists 3 different block numbers.
All inputs are finite; a program needn't handle non-finite values.
Results may differ from the reference program's by a relative error of at most 0.001.
Values may be sent and summed in bfloat16 or wider, within the bound.
A program may use at most 128 MiB of HBM per device.

```python
import math
import jax
import jax.numpy as jnp
import numpy as np
from jax import lax

D = 7168
FF = 1024
TOP = 2
TOK_DEV = 32
BLOCK = 128
DROP = 3
EXPERTS = 32
TOKENS = 4096
CAP = 3
NBLK = 8
KEEP = 5


def draw_dropped(key, part):
    key_list = jax.random.split(key, EXPERTS)
    shuffled = jax.vmap(lambda single_key: jax.random.permutation(single_key, NBLK))(key_list)
    return shuffled[:, :DROP].astype(jnp.int32)


def levels(key, extent, cuts, least, high):
    def one(position, shards_of):
        steps = jax.random.uniform(jax.random.fold_in(jax.random.fold_in(key, 6), position), (shards_of,), jnp.float32, least / len(cuts), high / len(cuts))
        return jnp.repeat(jnp.exp(steps), extent[position] // shards_of).reshape((-1,) + (1,) * (len(extent) - position - 1))

    loudness = one(*cuts[0])
    for cut in cuts[1:]:
        loudness = loudness * one(*cut)
    return loudness


def assign_block(stream_key, own, number, rows, number_of, top, most, skew):
    order = jax.random.permutation(stream_key, number_of)
    crowded, usual = portions_of(number_of, rows * top, most, skew, True), portions_of(number_of, rows * top, most, skew, False)
    places = jnp.arange(number_of)

    def named(sizes, rotation):
        used = int((sizes > 0).sum())
        fixed = max(1, used // 4)
        moved = fixed + (places - fixed + rotation * (used - fixed)) % max(1, number_of - fixed)
        return jnp.zeros((number_of,), jnp.int32).at[order[jnp.where(places < fixed, places, moved)]].set(jnp.asarray(sizes, jnp.int32))

    sizes = jnp.where(number % 4 == 0, named(crowded, number // 4), named(usual, number - number // 4 - 1))
    mixed = jax.random.permutation(jax.random.fold_in(own, 3), number_of)
    source_of, taker = mixed[0:number_of // 2 * 2:2], mixed[1:number_of // 2 * 2:2]
    room = jnp.minimum(sizes[source_of] - 1, most - sizes[taker]) // 2
    room = jnp.where((source_of == order[0]) | (taker == order[0]) | (sizes[taker] == 0), 0, jnp.maximum(room, 0))
    moved = jax.random.randint(jax.random.fold_in(own, 4), (number_of // 2,), 0, 1 << 20) % (room + 1)
    sizes = sizes.at[source_of].add(-moved).at[taker].add(moved)
    labels = jnp.searchsorted(jnp.cumsum(sizes), jnp.arange(rows * top), side="right").astype(jnp.int32)
    listing = labels.reshape(top, rows).T
    listing = listing[jax.random.permutation(jax.random.fold_in(own, 1), rows)]
    rotation = jax.random.randint(jax.random.fold_in(own, 2), (rows, 1), 0, top)
    return jnp.take_along_axis(listing, (jnp.arange(top)[None, :] + rotation) % top, axis=1)


def portions_of(number_of, total, reach, skew, full):
    loads = [(1 << 20) // math.isqrt(standing ** skew) + 1 for standing in range(1, number_of + 1)]
    largest = reach if full else min(reach, max(-(-total // number_of), total * loads[0] // sum(loads)))
    least = 1 if total - largest >= number_of - 1 else 0
    counts, surplus = [largest] + [least] * (number_of - 1), total - largest - least * (number_of - 1)
    while surplus > 0:
        candidates = [i for i in range(1, number_of) if counts[i] < largest] or [i for i in range(1, number_of) if counts[i] < reach]
        pool, budget = sum([loads[i] for i in candidates]), surplus
        for i in candidates:
            addition = min(reach - counts[i], max(1, budget * loads[i] // pool), surplus)
            counts[i] = counts[i] + addition
            surplus = surplus - addition
    return np.array(counts)


def noise(key, shape, spread, most, cuts=(), held_as=jnp.bfloat16):
    result = spread * jax.random.normal(key, shape, jnp.float32)
    if cuts:
        result = result * levels(key, shape, cuts, -0.22, 0.18)
    return jnp.clip(result, -most, most).astype(held_as)


def setup_inputs(seed: int = 0) -> dict:
    arg_keys = jax.random.split(jax.random.key(seed), 9)
    tokens = noise(arg_keys[0], (2, TOKENS, D), 1.0, 6.0, ((1, 128),))
    cotangent = noise(arg_keys[1], (2, TOKENS, D), 0.1, 0.625, ((1, 128),))
    route_gate = jnp.clip(0.19921875 + 0.80078125 * jax.random.uniform(arg_keys[2], (2, TOKENS, TOP), jnp.float32) ** levels(arg_keys[2], (2, TOKENS, TOP), ((1, 128),), -0.2, 0.2), 0.19921875, 1.0).astype(jnp.bfloat16)
    routes_keys = jax.random.split(jax.random.fold_in(arg_keys[3], 1), 2 * TOKENS // TOK_DEV)
    routes_turns = jax.random.permutation(jax.random.fold_in(arg_keys[3], 3), 2 * TOKENS // TOK_DEV)
    routes = jax.vmap(lambda own, number: assign_block(jax.random.fold_in(arg_keys[3], 2), own, number, TOK_DEV, EXPERTS, TOP, CAP, 2))(routes_keys, routes_turns).reshape((2, TOKENS, TOP))
    gate_weight = noise(arg_keys[4], (EXPERTS, D, FF), D ** -0.5, 0.0625, ((0, 32), (1, 4), (2, 4)))
    up_weight = noise(arg_keys[5], (EXPERTS, D, FF), D ** -0.5, 0.0625, ((0, 32), (1, 4), (2, 4)))
    down_weight = noise(arg_keys[6], (EXPERTS, FF, D), FF ** -0.5, 0.1875, ((0, 32), (1, 4), (2, 4)))
    dropped = draw_dropped(jax.random.fold_in(arg_keys[8], 71), 0)
    return dict(tokens=tokens, cotangent=cotangent, route_gate=route_gate, routes=routes, gate_weight=gate_weight, up_weight=up_weight, down_weight=down_weight, dropped=dropped)


def reference(tokens, cotangent, route_gate, routes, gate_weight, up_weight, down_weight, dropped):
    most_rows = TOKENS // TOK_DEV * CAP

    def one_expert(expert_id):
        def one_set(set_index):
            matched = routes[set_index] == expert_id
            weight_sum = jnp.sum(jnp.where(matched, route_gate[set_index].astype(jnp.float32), 0.0), axis=1)
            used = jnp.any(matched, axis=1)
            picked = jnp.nonzero(used, size=most_rows, fill_value=0)[0].astype(jnp.int32)
            valid = jnp.arange(most_rows, dtype=jnp.int32) < jnp.sum(used.astype(jnp.int32))
            rows_in = tokens[set_index][picked]
            gate_act = jnp.dot(rows_in, gate_weight[expert_id], preferred_element_type=jnp.float32)
            up_act = jnp.dot(rows_in, up_weight[expert_id], preferred_element_type=jnp.float32)
            hidden = jax.nn.silu(gate_act) * up_act
            scaled = jnp.where(valid, weight_sum[picked], 0.0)
            product = jnp.dot(cotangent[set_index][picked], down_weight[expert_id].T, preferred_element_type=jnp.float32)
            hidden_grad = scaled[:, None] * product
            return jnp.abs(jnp.sum(hidden * hidden_grad, axis=0))

        return jnp.stack([one_set(0), one_set(1)])

    per_expert = lax.map(one_expert, jnp.arange(EXPERTS, dtype=jnp.int32))
    saliency = jnp.transpose(per_expert, (1, 0, 2))

    blocks = jnp.arange(NBLK, dtype=jnp.int32)
    kept_flag = jnp.all(dropped[:, :, None] != blocks[None, None, :], axis=1)
    ranking = jnp.cumsum(kept_flag.astype(jnp.int32), axis=1) - 1
    slots_kept = jnp.arange(KEEP, dtype=jnp.int32)
    selected = kept_flag[:, None, :] & (ranking[:, None, :] == slots_kept[None, :, None])
    source_block = jnp.sum(jnp.where(selected, blocks[None, None, :], 0), axis=2).astype(jnp.int32)
    grouped = down_weight.reshape(EXPERTS, NBLK, BLOCK, D)
    gathered = jax.vmap(lambda group_rows, choice_rows: group_rows[choice_rows])(grouped, source_block)
    compact_down = gathered.reshape(EXPERTS, KEEP * BLOCK, D)
    return saliency, compact_down
```

```python
import jax
import jax.numpy as jnp
from jax import lax
from jax.sharding import PartitionSpec as P

BLOCK = 128
NBLK = 8
KEEP = 5


def slots_of(routes, capacity, experts):
    expert_ids = jnp.arange(experts, dtype=jnp.int32)
    matched = routes[..., None] == expert_ids
    chosen = jnp.any(matched, axis=-2).astype(jnp.float32)
    earlier = jnp.cumsum(chosen, axis=-2) - chosen
    return matched, chosen[..., None] * (earlier[..., None] == jnp.arange(capacity, dtype=jnp.float32))


def compaction(down_weight, dropped, tensor_pos, tensor_count):
    blocks = jnp.arange(NBLK, dtype=jnp.int32)
    kept_flag = jnp.all(dropped[0][:, None] != blocks[None, :], axis=0)
    ranking = jnp.cumsum(kept_flag.astype(jnp.int32)) - 1
    rows_out = KEEP * BLOCK // tensor_count
    whole_rows = lax.all_gather(down_weight, "tensor", axis=1, tiled=True)[0]
    target_rows = tensor_pos * rows_out + jnp.arange(rows_out, dtype=jnp.int32)
    wanted_rank = target_rows // BLOCK
    chosen_block = kept_flag[None, :] & (ranking[None, :] == wanted_rank[:, None])
    source_block = jnp.sum(jnp.where(chosen_block, blocks[None, :], 0), axis=1)
    source_rows = source_block * BLOCK + target_rows % BLOCK
    return jnp.take(whole_rows, source_rows, axis=0)[None]


def body(tokens, cotangent, route_gate, routes, gate_weight, up_weight, down_weight, dropped):
    experts = lax.axis_size("expert")
    dp = lax.axis_size("dp")
    tensor_count = lax.axis_size("tensor")
    tensor_pos = lax.axis_index("tensor")
    rows, width = tokens.shape[1], tokens.shape[2]
    top_count = routes.shape[2]
    capacity = min(rows, max(2, 3 * rows * top_count // (2 * experts)))
    own_set = tensor_pos % 2
    mine = lax.switch(
        tensor_pos,
        [lambda: tokens[0], lambda: tokens[1], lambda: cotangent[0], lambda: cotangent[1]],
    )
    part = lax.all_to_all(mine.reshape(rows, dp, width // dp), "dp", split_axis=1, concat_axis=0, tiled=True)
    part = part.reshape(dp, rows, width // dp)
    set_routes = lax.dynamic_index_in_dim(routes, own_set, 0, keepdims=False)
    all_routes = lax.all_gather(set_routes, "dp")
    _, placing = slots_of(all_routes, capacity, experts)
    packed = jnp.einsum(
        "ptec,ptd->epcd", placing.astype(jnp.bfloat16), part, preferred_element_type=jnp.float32
    ).astype(jnp.bfloat16)
    matched, own_placing = slots_of(routes, capacity, experts)
    weight_sum = jnp.sum(jnp.where(matched, route_gate.astype(jnp.float32)[:, :, :, None], 0.0), axis=2)
    slot_gate = jnp.einsum("stec,ste->esc", own_placing, weight_sum, precision=lax.Precision.HIGHEST)
    gates = lax.all_to_all(slot_gate.astype(jnp.bfloat16), "expert", split_axis=0, concat_axis=0, tiled=True)
    arrived = lax.all_to_all(packed, "expert", split_axis=0, concat_axis=0, tiled=True)
    every = lax.all_gather(arrived, "tensor")
    x_rows, grad_rows = every[:2], every[2:]
    gate_part = jnp.einsum("sepcd,df->psecf", x_rows, gate_weight[0], preferred_element_type=jnp.float32)
    up_part = jnp.einsum("sepcd,df->psecf", x_rows, up_weight[0], preferred_element_type=jnp.float32)
    grad_part = jnp.einsum("sepcd,fd->psecf", grad_rows, down_weight[0], preferred_element_type=jnp.float32)
    sums = jnp.sum(
        lax.all_to_all(
            jnp.stack([gate_part, up_part, grad_part], axis=1), "dp", split_axis=0, concat_axis=0, tiled=True
        ),
        axis=0,
    )
    hidden = jax.nn.silu(sums[0]) * sums[1]
    hidden_grad = jnp.transpose(gates.astype(jnp.float32), (1, 0, 2))[..., None] * sums[2]
    totals = lax.psum(jnp.sum(hidden * hidden_grad, axis=(1, 2)), "dp")
    saliency = jnp.abs(totals)[:, None, :]
    return (saliency, compaction(down_weight, dropped, tensor_pos, tensor_count))


def solution(mesh):
    return jax.shard_map(
        body,
        mesh=mesh,
        in_specs=(
            P(None, ("expert", "dp"), None),
            P(None, ("expert", "dp"), None),
            P(None, ("expert", "dp"), None),
            P(None, ("expert", "dp"), None),
            P("expert", "dp", "tensor"),
            P("expert", "dp", "tensor"),
            P("expert", "tensor", "dp"),
            P("expert", None),
        ),
        out_specs=(P(None, "expert", "tensor"), P("expert", "tensor", "dp")),
        check_vma=False,
    )
```

```python
import functools

import jax
import jax.numpy as jnp
from jax import lax
from jax.experimental import pallas as pl
from jax.experimental.pallas import tpu as pltpu
from jax.sharding import PartitionSpec as P

BLOCK = 128
NBLK = 8
KEEP = 5
CAP = 3
MESH = pl.DeviceIdType.MESH


def kernel(
    experts,
    tokens, cotangent, info, gate_w, up_w, down_w,
    out,
    mine, raw, info_own, info_all, packed, gate_send, gate_recv, arrived, wg, wu, wd, partial, sums, products, share, shares,
    local_sem, raw_send, raw_recv, info_send, info_recv, z_send, z_recv, g_send, g_recv,
    y_send, y_recv, f_send, f_recv, r_send, r_recv, s_send, s_recv,
):
    planes = experts // 2
    steps = planes // 2
    rows = tokens.shape[1]
    width = tokens.shape[2]
    lanes = width // 8
    slab = 8 * CAP // 8
    e = lax.axis_index("expert")
    p = lax.axis_index("dp")
    t = lax.axis_index("tensor")
    z = e // 2
    c = e % 2
    b = 2 * p + c

    def local(src, dst, sem):
        return pltpu.make_async_copy(src, dst, sem)

    def remote(src, dst, send, recv, expert, dp, tensor):
        return pltpu.make_async_remote_copy(
            src_ref=src, dst_ref=dst, send_sem=send, recv_sem=recv,
            device_id={"expert": expert, "dp": dp, "tensor": tensor}, device_id_type=MESH,
        )

    for index in range(4):
        source = tokens if index < 2 else cotangent

        @pl.when(t == index)
        def _():
            local(source.at[index % 2], mine, local_sem.at[0]).start()

    copies = [local(gate_w.at[0], wg, local_sem.at[1]), local(up_w.at[0], wu, local_sem.at[2]),
              local(down_w.at[0], wd, local_sem.at[3])]
    for copy in copies:
        copy.start()

    barrier = pltpu.get_barrier_semaphore()

    def greet(expert, dp, tensor):
        pl.semaphore_signal(
            barrier, inc=1, device_id={"expert": expert, "dp": dp, "tensor": tensor}, device_id_type=MESH
        )

    def greet_z(k, carry):
        greet((e + k) % experts, p, t)
        return carry

    lax.fori_loop(1, experts, greet_z, 0)
    for k in range(1, 4):
        greet(e, (p + k) % 4, t)
        greet(2 * z + 1 - c, (p + k) % 4, t)
        greet(e, p, (t + k) % 4)

    lane = lax.broadcasted_iota(jnp.int32, (2, 8, 128), 2)
    own_lanes = lane // rows == b % 4
    info_own[...] = jnp.where(own_lanes, info[...], 0.0)
    info_all[b] = info_own[...]
    local(tokens.at[0], mine, local_sem.at[0]).wait()
    pl.semaphore_wait(barrier, experts - 1 + 9)

    def raw_copy(k, other, owner):
        return remote(
            mine.at[:, pl.ds(pl.multiple_of(other * lanes, 128), lanes)], raw.at[owner],
            raw_send.at[k], raw_recv.at[k], 2 * z + other % 2, other // 2, t,
        )

    def info_copy(k, other, owner):
        return remote(
            info_own, info_all.at[owner], info_send.at[k], info_recv.at[k], 2 * z + other % 2, other // 2, t
        )

    own_raw = local(mine.at[:, pl.ds(pl.multiple_of(b * lanes, 128), lanes)], raw.at[b], local_sem.at[4])
    own_raw.start()
    for k in range(1, 8):
        info_copy(k, (b + k) % 8, b).start()
    for k in range(1, 8):
        raw_copy(k, (b + k) % 8, b).start()
    for k in range(1, 8):
        info_copy(k, (b + k) % 8, (b + 8 - k) % 8).wait_recv()

    count = 8 * rows

    def places(which):
        low = info_all[0, which] + info_all[1, which] + info_all[2, which] + info_all[3, which]
        high = info_all[4, which] + info_all[5, which] + info_all[6, which] + info_all[7, which]
        both = jnp.concatenate([low, high], axis=1)
        expert_of = lax.broadcasted_iota(jnp.int32, (experts, count), 0).astype(jnp.float32)
        first = jnp.broadcast_to(both[0:1], (experts, count)) == expert_of
        second = jnp.broadcast_to(both[1:2], (experts, count)) == expert_of
        chosen = jnp.where(first | second, 1.0, 0.0)
        above = lax.broadcasted_iota(jnp.int32, (count, count), 0)
        across = lax.broadcasted_iota(jnp.int32, (count, count), 1)
        before = jnp.where((above < across) & (above // rows == across // rows), 1.0, 0.0)
        rank = jnp.dot(
            chosen.astype(jnp.bfloat16), before.astype(jnp.bfloat16), preferred_element_type=jnp.float32
        )
        block_of = lax.broadcasted_iota(jnp.int32, (experts, count), 1) // rows
        place = jnp.where(chosen > 0.0, rank + CAP * block_of.astype(jnp.float32), -1.0)
        weight = jnp.where(first, jnp.broadcast_to(both[2:3], (experts, count)), 0.0) + jnp.where(
            second, jnp.broadcast_to(both[3:4], (experts, count)), 0.0
        )
        return place, weight

    group = 8
    slot_of = lax.broadcasted_iota(jnp.int32, (group, 8 * CAP, count), 1).astype(jnp.float32)

    def chosen_rows(place, start):
        part = place[start:start + group]
        return jnp.where(jnp.broadcast_to(part[:, None, :], slot_of.shape) == slot_of, 1.0, 0.0)

    place, _ = places(t % 2)
    for k in range(1, 8):
        raw_copy(k, (b + k) % 8, (b + 8 - k) % 8).wait_recv()
    own_raw.wait()
    whole = raw[...].reshape(count, lanes)
    for start in range(0, experts, group):
        select = chosen_rows(place, start).reshape(group * 8 * CAP, count).astype(jnp.bfloat16)
        values = jnp.dot(select, whole, preferred_element_type=jnp.float32)
        packed[slab * start:slab * (start + group)] = values.reshape(slab * group, 8, lanes).astype(jnp.bfloat16)

    def plane(i, sign):
        return (z + (i + 1 if sign else planes - (i + 1) % steps)) % planes

    def z_copy(i, sign, core, owner_core):
        expert = 2 * plane(i, sign) + core
        return remote(
            packed.at[pl.ds(expert * slab, slab)], arrived.at[i, t, sign, owner_core],
            z_send.at[i, sign, core], z_recv.at[i, sign, owner_core], expert, p, t,
        )

    def z_start(i, carry):
        for sign in range(2):
            for core in range(2):
                if sign == 1:
                    z_copy(i, 1, core, c).start()
                else:
                    @pl.when((i != steps - 1) | (c != core))
                    def _():
                        z_copy(i, 0, core, c).start()
        return carry

    own_slab = local(packed.at[pl.ds(e * slab, slab)], arrived.at[steps - 1, t, 0, c], z_recv.at[steps - 1, 0, c])
    own_slab.start()
    lax.fori_loop(0, steps, z_start, 0)

    gate_place, gate_weight = places(p % 2)
    row_at = lax.broadcasted_iota(jnp.int32, (group, 8 * CAP, 128), 1)
    lane_at = lax.broadcasted_iota(jnp.int32, (group, 8 * CAP, 128), 2)
    ones = jnp.ones((count, 128), jnp.bfloat16)
    for start in range(0, experts, group):
        part = gate_weight[start:start + group]
        weighted = chosen_rows(gate_place, start) * jnp.broadcast_to(part[:, None, :], slot_of.shape)
        spread = jnp.dot(
            weighted.reshape(group * 8 * CAP, count).astype(jnp.bfloat16), ones, preferred_element_type=jnp.float32
        ).reshape(group, 8 * CAP, 128)
        line = jnp.sum(jnp.where(row_at == lane_at, spread, 0.0), axis=1, keepdims=True)
        gate_send[start:start + group] = jnp.broadcast_to(line, (group, 8, 128))

    def g_copy(i, sign, core):
        expert = 2 * plane(i, sign) + core
        return remote(
            gate_send.at[expert], gate_recv.at[i], g_send.at[i, core], g_recv.at[i], expert, p, t
        )

    own_gate = local(gate_send.at[e], gate_recv.at[steps - 1], g_recv.at[steps - 1])

    def g_each(act):
        def g_step(i, carry):
            for core in range(2):
                @pl.when((c == 0) & (p // 2 == 1))
                def _():
                    act(g_copy(i, 1, core))

                @pl.when((c == 0) & (p // 2 == 0) & ((i != steps - 1) | (c != core)))
                def _():
                    act(g_copy(i, 0, core))
            return carry

        lax.fori_loop(0, steps, g_step, 0)

    g_each(lambda copy: copy.start())

    @pl.when((c == 0) & (p // 2 == 0))
    def _():
        own_gate.start()

    up_t, down_t, far_t = (t + 1) % 4, (t + 3) % 4, (t + 2) % 4

    def y_copy(i, way, owner):
        return remote(
            arrived.at[i, owner], arrived.at[i, owner], y_send.at[i, way], y_recv.at[i, way],
            e, p, up_t if way == 0 else down_t,
        )

    def f_copy(i, way, owner):
        return remote(
            arrived.at[i, owner, way], arrived.at[i, owner, way], f_send.at[i, way], f_recv.at[i, way],
            e, p, up_t if way == 0 else down_t,
        )

    def r_copy(i, k, owner):
        other = (p + k) % 4
        return remote(
            partial.at[i, other], sums.at[i, owner], r_send.at[i, k - 1], r_recv.at[i, k - 1], e, other, t
        )

    def take_z(i):
        for sign in range(2):
            for core in range(2):
                z_copy(i, sign, core, core).wait_recv()
        y_copy(i, 0, t).start()
        y_copy(i, 1, t).start()

    def take_y(i):
        y_copy(i, 0, down_t).wait_recv()
        f_copy(i, 0, down_t).start()
        y_copy(i, 1, up_t).wait_recv()
        f_copy(i, 1, up_t).start()

    def lhs(i, first, core):
        loaded = arrived[i, first:first + 2, :, core]
        return loaded.astype(jnp.float32).reshape(4 * 8 * CAP, lanes).astype(jnp.bfloat16)

    def multiply(i):
        f_copy(i, 0, far_t).wait_recv()
        f_copy(i, 1, far_t).wait_recv()
        low, high = lhs(i, 0, 0), lhs(i, 0, 1)
        grad_low, grad_high = lhs(i, 2, 0), lhs(i, 2, 1)

        def plain(weight):
            return jnp.dot(low, weight[:lanes], preferred_element_type=jnp.float32) + jnp.dot(
                high, weight[lanes:], preferred_element_type=jnp.float32
            )

        turned = (((1,), (1,)), ((), ()))
        results = (
            plain(wg),
            plain(wu),
            lax.dot_general(grad_low, wd[:, :lanes], turned, preferred_element_type=jnp.float32)
            + lax.dot_general(grad_high, wd[:, lanes:], turned, preferred_element_type=jnp.float32),
        )
        for index, value in enumerate(results):
            for which in range(2):
                for sign in range(2):
                    at = (2 * which + sign) * 8 * CAP
                    partial[i, 2 * sign + which, index] = value[at:at + 8 * CAP]
        for k in range(1, 4):
            r_copy(i, k, p).start()

    def finish(i):
        total = partial[i, p]
        for k in range(1, 4):
            r_copy(i, k, (p + 4 - k) % 4).wait_recv()
            total = total + sums[i, (p + 4 - k) % 4]
        hidden = total[0] / (1.0 + jnp.exp(-total[0])) * total[1]
        products[i] = hidden * total[2]

    for copy in copies:
        copy.wait()

    def step(s, carry):
        @pl.when((s >= 1) & (s < steps + 1))
        def _():
            take_y(s - 1)

        @pl.when(s < steps)
        def _():
            take_z(s)

        @pl.when((s >= 1) & (s < steps + 1))
        def _():
            multiply(s - 1)

        @pl.when(s >= 2)
        def _():
            finish(s - 2)
        return carry

    lax.fori_loop(0, steps + 2, step, 0)

    row24 = lax.broadcasted_iota(jnp.int32, (8 * CAP, 128), 0)
    lane24 = lax.broadcasted_iota(jnp.int32, (8 * CAP, 128), 1)

    def weigh(i, total):
        local(gate_send.at[e], gate_recv.at[i], g_recv.at[i]).wait()
        line = gate_recv[i]
        column = jnp.sum(
            jnp.where(row24 == lane24, jnp.broadcast_to(line[0:1], (8 * CAP, 128)), 0.0), axis=1, keepdims=True
        )
        return total + column * products[i]

    total = lax.fori_loop(0, steps, weigh, jnp.zeros((8 * CAP, products.shape[2]), jnp.float32))
    share[...] = jnp.broadcast_to(jnp.sum(total, axis=0, keepdims=True), share.shape)
    shares[p] = share[...]

    def s_copy(k, owner):
        return remote(share, shares.at[owner], s_send.at[k - 1], s_recv.at[k - 1], e, (p + k) % 4, t)

    for k in range(1, 4):
        s_copy(k, p).start()
    for k in range(1, 4):
        s_copy(k, (p + 4 - k) % 4).wait_recv()
    out[0] = jnp.abs(shares[0] + shares[2])
    out[1] = jnp.abs(shares[1] + shares[3])

    for k in range(1, 4):
        s_copy(k, p).wait_send()
    for k in range(1, 8):
        info_copy(k, (b + k) % 8, b).wait_send()
        raw_copy(k, (b + k) % 8, b).wait_send()
    g_each(lambda copy: copy.wait_send())

    def drain(i, carry):
        for sign in range(2):
            for core in range(2):
                if sign == 1:
                    z_copy(i, 1, core, c).wait_send()
                else:
                    @pl.when((i != steps - 1) | (c != core))
                    def _():
                        z_copy(i, 0, core, c).wait_send()
        for way in range(2):
            y_copy(i, way, t).wait_send()
            f_copy(i, way, down_t if way == 0 else up_t).wait_send()
        for k in range(1, 4):
            r_copy(i, k, p).wait_send()
        return carry

    lax.fori_loop(0, steps, drain, 0)


def routed(tokens, cotangent, info, gate_weight, up_weight, down_weight, experts):
    steps = experts // 4
    rows, width = tokens.shape[1:]
    lanes = width // 8
    depth, columns = gate_weight.shape[1:]
    slab = CAP
    anywhere = pl.BlockSpec(memory_space=pl.ANY)
    vmem = pl.BlockSpec(memory_space=pltpu.VMEM)
    half, full, dma = jnp.bfloat16, jnp.float32, pltpu.SemaphoreType.DMA
    return pl.pallas_call(
        functools.partial(kernel, experts),
        out_shape=jax.ShapeDtypeStruct((2, 8, columns), full),
        in_specs=[anywhere, anywhere, vmem, anywhere, anywhere, anywhere],
        out_specs=vmem,
        scratch_shapes=[
            pltpu.VMEM((rows, width), half),
            pltpu.VMEM((8, rows, lanes), half),
            pltpu.VMEM((2, 8, 128), full),
            pltpu.VMEM((8, 2, 8, 128), full),
            pltpu.VMEM((experts * slab, 8, lanes), half),
            pltpu.VMEM((experts, 8, 128), full),
            pltpu.VMEM((steps, 8, 128), full),
            pltpu.VMEM((steps, 4, 2, 2, slab, 8, lanes), half),
            pltpu.VMEM((depth, columns), half),
            pltpu.VMEM((depth, columns), half),
            pltpu.VMEM((columns, depth), half),
            pltpu.VMEM((steps, 4, 3, 8 * CAP, columns), full),
            pltpu.VMEM((steps, 4, 3, 8 * CAP, columns), full),
            pltpu.VMEM((steps, 8 * CAP, columns), full),
            pltpu.VMEM((8, columns), full),
            pltpu.VMEM((4, 8, columns), full),
            dma((5,)),
            dma((8,)), dma((8,)), dma((8,)), dma((8,)),
            dma((steps, 2, 2)), dma((steps, 2, 2)),
            dma((steps, 2)), dma((steps,)),
            dma((steps, 2)), dma((steps, 2)), dma((steps, 2)), dma((steps, 2)),
            dma((steps, 3)), dma((steps, 3)), dma((3,)), dma((3,)),
        ],
        compiler_params=pltpu.CompilerParams(
            collective_id=0, has_side_effects=True, vmem_limit_bytes=40 * 1024 * 1024
        ),
        cost_estimate=pl.CostEstimate(flops=4 * 10**9, transcendentals=10**5, bytes_accessed=2 * 10**8),
    )(tokens, cotangent, info, gate_weight, up_weight, down_weight)


def compaction(down_weight, dropped, tensor_pos, tensor_count):
    blocks = jnp.arange(NBLK, dtype=jnp.int32)
    kept_flag = jnp.all(dropped[0][:, None] != blocks[None, :], axis=0)
    ranking = jnp.cumsum(kept_flag.astype(jnp.int32)) - 1
    rows_out = KEEP * BLOCK // tensor_count
    whole_rows = lax.all_gather(down_weight, "tensor", axis=1, tiled=True)[0]
    target_rows = tensor_pos * rows_out + jnp.arange(rows_out, dtype=jnp.int32)
    wanted_rank = target_rows // BLOCK
    chosen_block = kept_flag[None, :] & (ranking[None, :] == wanted_rank[:, None])
    source_block = jnp.sum(jnp.where(chosen_block, blocks[None, :], 0), axis=1)
    source_rows = source_block * BLOCK + target_rows % BLOCK
    return jnp.take(whole_rows, source_rows, axis=0)[None]


def body(tokens, cotangent, route_gate, routes, gate_weight, up_weight, down_weight, dropped):
    experts = lax.axis_size("expert")
    tensor_count = lax.axis_size("tensor")
    tensor_pos = lax.axis_index("tensor")
    lines = jnp.concatenate([routes.astype(jnp.float32), route_gate.astype(jnp.float32)], axis=2)
    lines = jnp.transpose(lines, (0, 2, 1))
    info = jnp.pad(jnp.tile(lines, (1, 1, 4)), ((0, 0), (0, 4), (0, 0)))
    values = routed(tokens, cotangent, info, gate_weight, up_weight, down_weight, experts)
    saliency = values[:, :1]
    return (saliency, compaction(down_weight, dropped, tensor_pos, tensor_count))


def solution(mesh):
    return jax.shard_map(
        body,
        mesh=mesh,
        in_specs=(
            P(None, ("expert", "dp"), None),
            P(None, ("expert", "dp"), None),
            P(None, ("expert", "dp"), None),
            P(None, ("expert", "dp"), None),
            P("expert", "dp", "tensor"),
            P("expert", "dp", "tensor"),
            P("expert", "tensor", "dp"),
            P("expert", None),
        ),
        out_specs=(P(None, "expert", "tensor"), P("expert", "tensor", "dp")),
        check_vma=False,
    )
```

```python
import functools

import jax
import jax.numpy as jnp
from jax import lax
from jax.experimental import pallas as pl
from jax.experimental.pallas import tpu as pltpu
from jax.sharding import PartitionSpec as P

BLOCK = 128
KEEP = 5
CAP = 3
MESH = pl.DeviceIdType.MESH
UNIT = 32
WINDOW = 3
OFFERS = ((0, 1, 5, 3), (1, 0, 0, 5), (1, 2, 10, 5), (1, 3, 15, 1), (2, 0, 4, 1), (2, 1, 5, 5), (2, 3, 15, 5), (3, 2, 12, 3))
HOLDERS = ((0, 1), (0, 1, 2), (1, 2), (1, 2, 3), (2, 3))


def kernel(
    experts,
    tokens, cotangent, routes, route_gate, dropped, gate_w, up_w, down_w,
    out, compact,
    mine, own_routes, own_gates, raw, info_own, info_all, packed, gate_send, gate_recv, arrived, wg, wu, wd, partial, sums, acc, share, shares, offered, taken,
    local_sem, raw_send, raw_recv, info_send, info_recv, z_send, z_recv, g_send, g_recv,
    y_send, y_recv, f_send, f_recv, r_send, r_recv, s_send, s_recv, c_send, c_recv,
):
    planes = experts // 2
    steps = planes // 2
    rows = tokens.shape[1]
    width = tokens.shape[2]
    lanes = width // 8
    slab = 8 * CAP // 8
    e = lax.axis_index("expert")
    p = lax.axis_index("dp")
    t = lax.axis_index("tensor")
    z = e // 2
    c = e % 2
    b = 2 * p + c

    def local(src, dst, sem):
        return pltpu.make_async_copy(src, dst, sem)

    def remote(src, dst, send, recv, expert, dp, tensor):
        return pltpu.make_async_remote_copy(
            src_ref=src, dst_ref=dst, send_sem=send, recv_sem=recv,
            device_id={"expert": expert, "dp": dp, "tensor": tensor}, device_id_type=MESH,
        )

    for index in range(4):
        source = tokens if index < 2 else cotangent

        @pl.when(t == index)
        def _():
            local(source.at[index % 2], mine, local_sem.at[0]).start()

    copies = [local(gate_w.at[0], wg, local_sem.at[1]), local(up_w.at[0], wu, local_sem.at[2]),
              local(down_w.at[0], wd, local_sem.at[3])]
    small = [local(routes, own_routes, local_sem.at[5]), local(route_gate, own_gates, local_sem.at[6])]
    for copy in small:
        copy.start()
    for copy in copies:
        copy.start()

    barrier = pltpu.get_barrier_semaphore()

    def greet(expert, dp, tensor):
        pl.semaphore_signal(
            barrier, inc=1, device_id={"expert": expert, "dp": dp, "tensor": tensor}, device_id_type=MESH
        )

    def greet_z(k, carry):
        greet((e + k) % experts, p, t)
        return carry

    lax.fori_loop(1, experts, greet_z, 0)
    for k in range(1, 4):
        greet(e, (p + k) % 4, t)
        greet(2 * z + 1 - c, (p + k) % 4, t)
        greet(e, p, (t + k) % 4)

    for copy in small:
        copy.wait()
    lane = lax.broadcasted_iota(jnp.int32, (2, 128), 1)
    own_lanes = lane // rows == b % 4
    spread_of = jnp.where(
        lax.broadcasted_iota(jnp.int32, (rows, 128), 0) == lax.broadcasted_iota(jnp.int32, (rows, 128), 1) % rows, 1.0, 0.0
    ).astype(jnp.bfloat16)
    info_own[...] = jnp.zeros(info_own.shape, jnp.float32)
    for which in range(2):
        for at, lines in ((0, own_routes[which].astype(jnp.float32)), (2, own_gates[which].astype(jnp.float32))):
            wide = jnp.dot(lines.astype(jnp.bfloat16), spread_of, preferred_element_type=jnp.float32)
            info_own[which, at:at + 2] = jnp.where(own_lanes, wide, 0.0)
    info_all[b] = info_own[...]
    first, second, third = dropped[0, 0], dropped[0, 1], dropped[0, 2]
    least = jnp.minimum(first, jnp.minimum(second, third))
    most = jnp.maximum(first, jnp.maximum(second, third))
    middle = first + second + third - least - most
    kept = []
    for rank in range(KEEP):
        number = jnp.where(least <= rank, rank + 1, rank)
        number = jnp.where(middle <= number, number + 1, number)
        kept.append(jnp.where(most <= number, number + 1, number))
    copies[2].wait()
    for rank in range(KEEP):
        offered[rank * BLOCK:(rank + 1) * BLOCK] = jnp.where(kept[rank] == 2 * t, wd[:BLOCK], wd[BLOCK:])
    local(tokens.at[0], mine, local_sem.at[0]).wait()
    pl.semaphore_wait(barrier, experts - 1 + 9)

    def raw_copy(k, other, owner):
        return remote(
            mine.at[:, pl.ds(pl.multiple_of(other * lanes, 128), lanes)], raw.at[owner],
            raw_send.at[k], raw_recv.at[k], 2 * z + other % 2, other // 2, t,
        )

    def info_copy(k, other, owner):
        return remote(
            info_own, info_all.at[owner], info_send.at[k], info_recv.at[k], 2 * z + other % 2, other // 2, t
        )

    own_raw = local(mine.at[:, pl.ds(pl.multiple_of(b * lanes, 128), lanes)], raw.at[b], local_sem.at[4])
    own_raw.start()
    for k in range(1, 8):
        info_copy(k, (b + k) % 8, b).start()
    for k in range(1, 8):
        raw_copy(k, (b + k) % 8, b).start()

    def offer(holder, taker, start, size):
        away = (taker - holder) % 4 - 1
        return remote(
            offered.at[pl.ds(start * UNIT, size * UNIT)], taken.at[away, pl.ds((start - KEEP * taker) * UNIT, size * UNIT)],
            c_send.at[away], c_recv.at[away], e, p, taker,
        )

    def each_offer(act):
        for entry in OFFERS:
            @pl.when(t == entry[0])
            def _():
                act(offer(*entry))

    each_offer(lambda copy: copy.start())
    for k in range(1, 8):
        info_copy(k, (b + k) % 8, (b + 8 - k) % 8).wait_recv()

    count = 8 * rows

    def places(which):
        low = info_all[0, which] + info_all[1, which] + info_all[2, which] + info_all[3, which]
        high = info_all[4, which] + info_all[5, which] + info_all[6, which] + info_all[7, which]
        both = jnp.concatenate([low, high], axis=1)
        expert_of = lax.broadcasted_iota(jnp.int32, (experts, count), 0).astype(jnp.float32)
        first = jnp.broadcast_to(both[0:1], (experts, count)) == expert_of
        second = jnp.broadcast_to(both[1:2], (experts, count)) == expert_of
        chosen = jnp.where(first | second, 1.0, 0.0)
        above = lax.broadcasted_iota(jnp.int32, (count, count), 0)
        across = lax.broadcasted_iota(jnp.int32, (count, count), 1)
        before = jnp.where((above < across) & (above // rows == across // rows), 1.0, 0.0)
        rank = jnp.dot(
            chosen.astype(jnp.bfloat16), before.astype(jnp.bfloat16), preferred_element_type=jnp.float32
        )
        block_of = lax.broadcasted_iota(jnp.int32, (experts, count), 1) // rows
        place = jnp.where(chosen > 0.0, rank + CAP * block_of.astype(jnp.float32), -1.0)
        weight = jnp.where(first, jnp.broadcast_to(both[2:3], (experts, count)), 0.0) + jnp.where(
            second, jnp.broadcast_to(both[3:4], (experts, count)), 0.0
        )
        return place, weight

    group = 8
    slot_of = lax.broadcasted_iota(jnp.int32, (group, 8 * CAP, count), 1).astype(jnp.float32)

    def chosen_rows(place, start):
        part = place[start:start + group]
        return jnp.where(jnp.broadcast_to(part[:, None, :], slot_of.shape) == slot_of, 1.0, 0.0)

    place, _ = places(t % 2)
    for k in range(1, 8):
        raw_copy(k, (b + k) % 8, (b + 8 - k) % 8).wait_recv()
    own_raw.wait()
    whole = raw[...].reshape(count, lanes)
    for start in range(0, experts, group):
        select = chosen_rows(place, start).reshape(group * 8 * CAP, count).astype(jnp.bfloat16)
        values = jnp.dot(select, whole, preferred_element_type=jnp.float32)
        packed[slab * start:slab * (start + group)] = values.reshape(slab * group, 8, lanes).astype(jnp.bfloat16)

    def plane(i, sign):
        return (z + (i + 1 if sign else planes - (i + 1) % steps)) % planes

    def z_copy(i, sign, core, owner_core):
        expert = 2 * plane(i, sign) + core
        return remote(
            packed.at[pl.ds(expert * slab, slab)], arrived.at[i, t, sign, owner_core],
            z_send.at[i, sign, core], z_recv.at[i, sign, owner_core], expert, p, t,
        )

    def z_start(i, carry):
        for sign in range(2):
            for core in range(2):
                if sign == 1:
                    z_copy(i, 1, core, c).start()
                else:
                    @pl.when(i != steps - 1)
                    def _():
                        z_copy(i, 0, core, c).start()
        return carry

    def z_sent(i):
        for sign in range(2):
            for core in range(2):
                if sign == 1:
                    z_copy(i, 1, core, c).wait_send()
                else:
                    @pl.when((i != steps - 1) | (c != core))
                    def _():
                        z_copy(i, 0, core, c).wait_send()

    own_slab = local(packed.at[pl.ds(e * slab, slab)], arrived.at[steps - 1, t, 0, c], z_recv.at[steps - 1, 0, c])
    own_slab.start()
    for core in range(2):
        @pl.when(c != core)
        def _():
            z_copy(steps - 1, 0, core, c).start()
    lax.fori_loop(0, min(WINDOW, steps), z_start, 0)

    gate_place, gate_weight = places(p % 2)
    row_at = lax.broadcasted_iota(jnp.int32, (group, 8 * CAP, 128), 1)
    lane_at = lax.broadcasted_iota(jnp.int32, (group, 8 * CAP, 128), 2)
    ones = jnp.ones((count, 128), jnp.bfloat16)
    for start in range(0, experts, group):
        part = gate_weight[start:start + group]
        weighted = chosen_rows(gate_place, start) * jnp.broadcast_to(part[:, None, :], slot_of.shape)
        spread = jnp.dot(
            weighted.reshape(group * 8 * CAP, count).astype(jnp.bfloat16), ones, preferred_element_type=jnp.float32
        ).reshape(group, 8 * CAP, 128)
        line = jnp.sum(jnp.where(row_at == lane_at, spread, 0.0), axis=1, keepdims=True)
        gate_send[start:start + group] = line

    def g_copy(i, sign, core):
        expert = 2 * plane(i, sign) + core
        return remote(
            gate_send.at[expert], gate_recv.at[i], g_send.at[i, core], g_recv.at[i], expert, p, t
        )

    own_gate = local(gate_send.at[e], gate_recv.at[steps - 1], g_recv.at[steps - 1])

    def g_each(act):
        def g_step(i, carry):
            for core in range(2):
                @pl.when((c == 0) & (p // 2 == 1))
                def _():
                    act(g_copy(i, 1, core))

                @pl.when((c == 0) & (p // 2 == 0) & ((i != steps - 1) | (c != core)))
                def _():
                    act(g_copy(i, 0, core))
            return carry

        lax.fori_loop(0, steps, g_step, 0)

    g_each(lambda copy: copy.start())

    @pl.when((c == 0) & (p // 2 == 0))
    def _():
        own_gate.start()

    up_t, down_t, far_t = (t + 1) % 4, (t + 3) % 4, (t + 2) % 4

    def y_copy(i, sign, way, owner):
        return remote(
            arrived.at[i, owner, sign], arrived.at[i, owner, sign], y_send.at[i, sign, way], y_recv.at[i, sign, way],
            e, p, up_t if way == 0 else down_t,
        )

    def f_copy(i, way, owner):
        return remote(
            arrived.at[i, owner, way], arrived.at[i, owner, way], f_send.at[i, way], f_recv.at[i, way],
            e, p, up_t if way == 0 else down_t,
        )

    def r_copy(i, k, owner):
        other = (p + k) % 4
        return remote(
            partial.at[i, other], sums.at[i, owner], r_send.at[i, k - 1], r_recv.at[i, k - 1], e, other, t
        )

    def take_z(i, sign):
        for core in range(2):
            z_copy(i, sign, core, core).wait_recv()
        y_copy(i, sign, 0, t).start()
        y_copy(i, sign, 1, t).start()

    def take_y(i, sign):
        owner = down_t if sign == 0 else up_t
        y_copy(i, sign, sign, owner).wait_recv()
        f_copy(i, sign, owner).start()

    def take_compact():
        for entry in OFFERS:
            @pl.when(t == entry[1])
            def _():
                offer(*entry).wait_recv()
        for taker in range(4):
            @pl.when(t == taker)
            def _():
                for unit in range(KEEP):
                    rank = (KEEP * taker + unit) // 4
                    at = (KEEP * taker + unit) * UNIT
                    value = offered[at:at + UNIT]
                    for holder in HOLDERS[rank]:
                        if holder != taker:
                            other = taken[(taker - holder) % 4 - 1, unit * UNIT:(unit + 1) * UNIT]
                            value = jnp.where(kept[rank] // 2 == holder, other, value)
                    compact[0, unit * UNIT:(unit + 1) * UNIT] = value

    def lhs(i, first, core):
        loaded = arrived[i, first:first + 2, :, core]
        return loaded.astype(jnp.float32).reshape(4 * 8 * CAP, lanes).astype(jnp.bfloat16)

    def multiply(i):
        f_copy(i, 0, far_t).wait_recv()
        f_copy(i, 1, far_t).wait_recv()
        y_copy(i, 0, 1, up_t).wait_recv()
        y_copy(i, 1, 0, down_t).wait_recv()
        low, high = lhs(i, 0, 0), lhs(i, 0, 1)
        grad_low, grad_high = lhs(i, 2, 0), lhs(i, 2, 1)

        def plain(weight):
            return jnp.dot(low, weight[:lanes], preferred_element_type=jnp.float32) + jnp.dot(
                high, weight[lanes:], preferred_element_type=jnp.float32
            )

        turned = (((1,), (1,)), ((), ()))
        results = (
            plain(wg),
            plain(wu),
            lax.dot_general(grad_low, wd[:, :lanes], turned, preferred_element_type=jnp.float32)
            + lax.dot_general(grad_high, wd[:, lanes:], turned, preferred_element_type=jnp.float32),
        )
        for index, value in enumerate(results):
            for which in range(2):
                for sign in range(2):
                    at = (2 * which + sign) * 8 * CAP
                    partial[i, 2 * sign + which, index] = value[at:at + 8 * CAP]
        for k in range(1, 4):
            r_copy(i, k, p).start()

    def finish(i):
        total = partial[i, p]
        for k in range(1, 4):
            r_copy(i, k, (p + 4 - k) % 4).wait_recv()
            total = total + sums[i, (p + 4 - k) % 4]
        hidden = total[0] / (1.0 + jnp.exp(-total[0])) * total[1]
        local(gate_send.at[e], gate_recv.at[i], g_recv.at[i]).wait()
        column = jnp.sum(
            jnp.where(row24 == lane24, jnp.broadcast_to(gate_recv[i], (8 * CAP, 128)), 0.0), axis=1, keepdims=True
        )
        acc[...] += column * hidden * total[2]

    for copy in copies[:2]:
        copy.wait()
    row24 = lax.broadcasted_iota(jnp.int32, (8 * CAP, 128), 0)
    lane24 = lax.broadcasted_iota(jnp.int32, (8 * CAP, 128), 1)
    acc[...] = jnp.zeros(acc.shape, jnp.float32)
    take_z(steps - 1, 0)

    def step(s, carry):
        @pl.when(s == 1)
        def _():
            take_y(steps - 1, 0)

        @pl.when((s >= 1) & (s < steps))
        def _():
            take_y(s - 1, 0)

        @pl.when((s >= 1) & (s < steps + 1))
        def _():
            take_y(s - 1, 1)

        @pl.when(s < steps - 1)
        def _():
            take_z(s, 0)

        @pl.when(s < steps)
        def _():
            take_z(s, 1)

        @pl.when(s < steps - WINDOW)
        def _():
            z_sent(s)
            z_start(s + WINDOW, 0)

        @pl.when((s >= 1) & (s < steps + 1))
        def _():
            multiply(s - 1)

        @pl.when(s >= 2)
        def _():
            finish(s - 2)

        @pl.when(s == steps // 2)
        def _():
            take_compact()
        return carry

    lax.fori_loop(0, steps + 2, step, 0)
    total = acc[...]
    share[...] = jnp.broadcast_to(jnp.sum(total, axis=0, keepdims=True), share.shape)
    shares[p] = share[...]

    def s_copy(k, owner):
        return remote(share, shares.at[owner], s_send.at[k - 1], s_recv.at[k - 1], e, (p + k) % 4, t)

    for k in range(1, 4):
        s_copy(k, p).start()
    for k in range(1, 4):
        s_copy(k, (p + 4 - k) % 4).wait_recv()
    out[0] = jnp.abs(shares[0] + shares[2])
    out[1] = jnp.abs(shares[1] + shares[3])

    for k in range(1, 4):
        s_copy(k, p).wait_send()
    for k in range(1, 8):
        info_copy(k, (b + k) % 8, b).wait_send()
        raw_copy(k, (b + k) % 8, b).wait_send()
    g_each(lambda copy: copy.wait_send())

    each_offer(lambda copy: copy.wait_send())

    def drain(i, carry):
        @pl.when(i >= steps - WINDOW)
        def _():
            z_sent(i)

        for way in range(2):
            for sign in range(2):
                y_copy(i, sign, way, t).wait_send()
            f_copy(i, way, down_t if way == 0 else up_t).wait_send()
        for k in range(1, 4):
            r_copy(i, k, p).wait_send()
        return carry

    lax.fori_loop(0, steps, drain, 0)


def routed(tokens, cotangent, routes, route_gate, dropped, gate_weight, up_weight, down_weight, experts):
    steps = experts // 4
    rows, width = tokens.shape[1:]
    lanes = width // 8
    depth, columns = gate_weight.shape[1:]
    slab = CAP
    anywhere = pl.BlockSpec(memory_space=pltpu.HBM)
    vmem = pl.BlockSpec(memory_space=pltpu.VMEM)
    half, full, dma = jnp.bfloat16, jnp.float32, pltpu.SemaphoreType.DMA
    return pl.pallas_call(
        functools.partial(kernel, experts),
        out_shape=(
            jax.ShapeDtypeStruct((2, 1, columns), full),
            jax.ShapeDtypeStruct((1, KEEP * UNIT, depth), half),
        ),
        in_specs=[anywhere] * 4 + [pl.BlockSpec(memory_space=pltpu.SMEM)] + [anywhere] * 3,
        out_specs=(vmem, vmem),
        scratch_shapes=[
            pltpu.VMEM((rows, width), half),
            pltpu.VMEM((2, 2, rows), jnp.int32),
            pltpu.VMEM((2, 2, rows), half),
            pltpu.VMEM((8, rows, lanes), half),
            pltpu.VMEM((2, 8, 128), full),
            pltpu.VMEM((8, 2, 8, 128), full),
            pltpu.VMEM((experts * slab, 8, lanes), half),
            pltpu.VMEM((experts, 1, 128), full),
            pltpu.VMEM((steps, 1, 128), full),
            pltpu.VMEM((steps, 4, 2, 2, slab, 8, lanes), half),
            pltpu.VMEM((depth, columns), half),
            pltpu.VMEM((depth, columns), half),
            pltpu.VMEM((columns, depth), half),
            pltpu.VMEM((steps, 4, 3, 8 * CAP, columns), full),
            pltpu.VMEM((steps, 4, 3, 8 * CAP, columns), full),
            pltpu.VMEM((8 * CAP, columns), full),
            pltpu.VMEM((1, columns), full),
            pltpu.VMEM((4, 1, columns), full),
            pltpu.VMEM((KEEP * BLOCK, depth), half),
            pltpu.VMEM((3, KEEP * UNIT, depth), half),
            dma((7,)),
            dma((8,)), dma((8,)), dma((8,)), dma((8,)),
            dma((steps, 2, 2)), dma((steps, 2, 2)),
            dma((steps, 2)), dma((steps,)),
            dma((steps, 2, 2)), dma((steps, 2, 2)), dma((steps, 2)), dma((steps, 2)),
            dma((steps, 3)), dma((steps, 3)), dma((3,)), dma((3,)), dma((3,)), dma((3,)),
        ],
        compiler_params=pltpu.CompilerParams(
            collective_id=0, has_side_effects=True, vmem_limit_bytes=40 * 1024 * 1024
        ),
        cost_estimate=pl.CostEstimate(flops=4 * 10**9, transcendentals=10**5, bytes_accessed=2 * 10**8),
    )(tokens, cotangent, routes, route_gate, dropped, gate_weight, up_weight, down_weight)


def body(tokens, cotangent, route_gate, routes, gate_weight, up_weight, down_weight, dropped):
    return routed(
        tokens, cotangent, jnp.transpose(routes, (0, 2, 1)), jnp.transpose(route_gate, (0, 2, 1)), dropped,
        gate_weight, up_weight, down_weight, lax.axis_size("expert"),
    )


def solution(mesh):
    return jax.shard_map(
        body,
        mesh=mesh,
        in_specs=(
            P(None, ("expert", "dp"), None),
            P(None, ("expert", "dp"), None),
            P(None, ("expert", "dp"), None),
            P(None, ("expert", "dp"), None),
            P("expert", "dp", "tensor"),
            P("expert", "dp", "tensor"),
            P("expert", "tensor", "dp"),
            P("expert", None),
        ),
        out_specs=(P(None, "expert", "tensor"), P("expert", "tensor", "dp")),
        check_vma=False,
    )
```

```python
import functools

import jax
import jax.numpy as jnp
from jax import lax
from jax.experimental import pallas as pl
from jax.experimental.pallas import tpu as pltpu
from jax.sharding import PartitionSpec as P

BLOCK = 128
KEEP = 5
CAP = 3
MESH = pl.DeviceIdType.MESH
UNIT = 32
WINDOW = 3
OFFERS = ((0, 1, 5, 3), (1, 0, 0, 5), (1, 2, 10, 5), (1, 3, 15, 1), (2, 0, 4, 1), (2, 1, 5, 5), (2, 3, 15, 5), (3, 2, 12, 3))
HOLDERS = ((0, 1), (0, 1, 2), (1, 2), (1, 2, 3), (2, 3))


def kernel(
    experts,
    tokens, cotangent, routes, route_gate, dropped, gate_w, up_w, down_w,
    out, compact_out,
    mine, own_routes, own_gates, raw, info_own, info_all, packed, gate_send, gate_recv, arrived, wg, wu, wd, wdt, partial, sums, acc, share, shares, offered, taken, compact,
    local_sem, raw_send, raw_recv, info_send, info_recv, z_send, z_recv, g_send, g_recv,
    y_send, y_recv, f_send, f_recv, r_send, r_recv, s_send, s_recv, c_send, c_recv,
):
    planes = experts // 2
    steps = planes // 2
    rows = tokens.shape[1]
    width = tokens.shape[2]
    lanes = width // 8
    slab = 8 * CAP // 8
    e = lax.axis_index("expert")
    p = lax.axis_index("dp")
    t = lax.axis_index("tensor")
    z = e // 2
    c = e % 2
    b = 2 * p + c

    def local(src, dst, sem):
        return pltpu.make_async_copy(src, dst, sem)

    def remote(src, dst, send, recv, expert, dp, tensor):
        return pltpu.make_async_remote_copy(
            src_ref=src, dst_ref=dst, send_sem=send, recv_sem=recv,
            device_id={"expert": expert, "dp": dp, "tensor": tensor}, device_id_type=MESH,
        )

    barrier = pltpu.get_barrier_semaphore()

    def greet(expert, dp, tensor):
        pl.semaphore_signal(
            barrier, inc=1, device_id={"expert": expert, "dp": dp, "tensor": tensor}, device_id_type=MESH
        )

    def greet_z(k, carry):
        greet((e + k) % experts, p, t)
        return carry

    lax.fori_loop(1, experts, greet_z, 0)
    for k in range(1, 4):
        greet(e, (p + k) % 4, t)
        greet(2 * z + 1 - c, (p + k) % 4, t)
        greet(e, p, (t + k) % 4)

    for index in range(4):
        source = tokens if index < 2 else cotangent

        @pl.when(t == index)
        def _():
            local(source.at[index % 2], mine, local_sem.at[0]).start()

    copies = [local(gate_w.at[0], wg, local_sem.at[1]), local(up_w.at[0], wu, local_sem.at[2]),
              local(down_w.at[0], wd, local_sem.at[3])]
    small = [local(routes, own_routes, local_sem.at[5]), local(route_gate, own_gates, local_sem.at[6])]
    for copy in small:
        copy.start()
    for copy in copies:
        copy.start()

    for copy in small:
        copy.wait()
    lane = lax.broadcasted_iota(jnp.int32, (2, 128), 1)
    own_lanes = lane // rows == b % 4
    spread_of = jnp.where(
        lax.broadcasted_iota(jnp.int32, (rows, 128), 0) == lax.broadcasted_iota(jnp.int32, (rows, 128), 1) % rows, 1.0, 0.0
    ).astype(jnp.bfloat16)
    info_own[...] = jnp.zeros(info_own.shape, jnp.float32)
    for which in range(2):
        for at, lines in ((0, own_routes[which].astype(jnp.float32)), (2, own_gates[which].astype(jnp.float32))):
            wide = jnp.dot(lines.astype(jnp.bfloat16), spread_of, preferred_element_type=jnp.float32)
            info_own[which, at:at + 2] = jnp.where(own_lanes, wide, 0.0)
    info_all[b] = info_own[...]
    local(tokens.at[0], mine, local_sem.at[0]).wait()
    pl.semaphore_wait(barrier, experts - 1 + 9)

    def raw_copy(k, other, owner):
        return remote(
            mine.at[:, pl.ds(pl.multiple_of(other * lanes, 128), lanes)], raw.at[owner],
            raw_send.at[k], raw_recv.at[k], 2 * z + other % 2, other // 2, t,
        )

    def info_copy(k, other, owner):
        return remote(
            info_own, info_all.at[owner], info_send.at[k], info_recv.at[k], 2 * z + other % 2, other // 2, t
        )

    own_raw = local(mine.at[:, pl.ds(pl.multiple_of(b * lanes, 128), lanes)], raw.at[b], local_sem.at[4])
    own_raw.start()
    for k in range(1, 8):
        info_copy(k, (b + k) % 8, b).start()
    for k in range(1, 8):
        raw_copy(k, (b + k) % 8, b).start()

    first, second, third = dropped[0, 0], dropped[0, 1], dropped[0, 2]
    least = jnp.minimum(first, jnp.minimum(second, third))
    most = jnp.maximum(first, jnp.maximum(second, third))
    middle = first + second + third - least - most
    kept = []
    for rank in range(KEEP):
        number = jnp.where(least <= rank, rank + 1, rank)
        number = jnp.where(middle <= number, number + 1, number)
        kept.append(jnp.where(most <= number, number + 1, number))
    copies[2].wait()
    for rank in range(KEEP):
        offered[rank * BLOCK:(rank + 1) * BLOCK] = jnp.where(kept[rank] == 2 * t, wd[:BLOCK], wd[BLOCK:])

    def offer(holder, taker, start, size):
        away = (taker - holder) % 4 - 1
        return remote(
            offered.at[pl.ds(start * UNIT, size * UNIT)], taken.at[away, pl.ds((start - KEEP * taker) * UNIT, size * UNIT)],
            c_send.at[away], c_recv.at[away], e, p, taker,
        )

    def each_offer(act):
        for entry in OFFERS:
            @pl.when(t == entry[0])
            def _():
                act(offer(*entry))

    each_offer(lambda copy: copy.start())
    for k in range(1, 8):
        info_copy(k, (b + k) % 8, (b + 8 - k) % 8).wait_recv()

    count = 8 * rows

    def places(which):
        low = info_all[0, which] + info_all[1, which] + info_all[2, which] + info_all[3, which]
        high = info_all[4, which] + info_all[5, which] + info_all[6, which] + info_all[7, which]
        both = jnp.concatenate([low, high], axis=1)
        expert_of = lax.broadcasted_iota(jnp.int32, (experts, count), 0).astype(jnp.float32)
        first = jnp.broadcast_to(both[0:1], (experts, count)) == expert_of
        second = jnp.broadcast_to(both[1:2], (experts, count)) == expert_of
        chosen = jnp.where(first | second, 1.0, 0.0)
        above = lax.broadcasted_iota(jnp.int32, (count, count), 0)
        across = lax.broadcasted_iota(jnp.int32, (count, count), 1)
        before = jnp.where((above < across) & (above // rows == across // rows), 1.0, 0.0)
        rank = jnp.dot(
            chosen.astype(jnp.bfloat16), before.astype(jnp.bfloat16), preferred_element_type=jnp.float32
        )
        block_of = lax.broadcasted_iota(jnp.int32, (experts, count), 1) // rows
        place = jnp.where(chosen > 0.0, rank + CAP * block_of.astype(jnp.float32), -1.0)
        weight = jnp.where(first, jnp.broadcast_to(both[2:3], (experts, count)), 0.0) + jnp.where(
            second, jnp.broadcast_to(both[3:4], (experts, count)), 0.0
        )
        return place, weight

    group = 8
    slot_of = lax.broadcasted_iota(jnp.int32, (group, 8 * CAP, count), 1).astype(jnp.float32)

    def chosen_rows(place, start):
        part = place[start:start + group]
        return jnp.where(jnp.broadcast_to(part[:, None, :], slot_of.shape) == slot_of, 1.0, 0.0)

    place, _ = places(t % 2)
    for k in range(1, 8):
        raw_copy(k, (b + k) % 8, (b + 8 - k) % 8).wait_recv()
    own_raw.wait()
    whole = raw[...].reshape(count, lanes)
    for start in range(0, experts, group):
        select = chosen_rows(place, start).reshape(group * 8 * CAP, count).astype(jnp.bfloat16)
        values = jnp.dot(select, whole, preferred_element_type=jnp.float32)
        packed[slab * start:slab * (start + group)] = values.reshape(slab * group, 8, lanes).astype(jnp.bfloat16)

    def plane(i, sign):
        return (z + (i + 1 if sign else planes - (i + 1) % steps)) % planes

    def z_copy(i, sign, core, owner_core):
        expert = 2 * plane(i, sign) + core
        return remote(
            packed.at[pl.ds(expert * slab, slab)], arrived.at[i, t, sign, owner_core],
            z_send.at[i, sign, core], z_recv.at[i, sign, owner_core], expert, p, t,
        )

    def z_start(i, carry):
        for sign in range(2):
            for core in range(2):
                if sign == 1:
                    z_copy(i, 1, core, c).start()
                else:
                    @pl.when(i != steps - 1)
                    def _():
                        z_copy(i, 0, core, c).start()
        return carry

    def z_sent(i):
        for sign in range(2):
            for core in range(2):
                if sign == 1:
                    z_copy(i, 1, core, c).wait_send()
                else:
                    @pl.when((i != steps - 1) | (c != core))
                    def _():
                        z_copy(i, 0, core, c).wait_send()

    own_slab = local(packed.at[pl.ds(e * slab, slab)], arrived.at[steps - 1, t, 0, c], z_recv.at[steps - 1, 0, c])
    own_slab.start()
    for core in range(2):
        @pl.when(c != core)
        def _():
            z_copy(steps - 1, 0, core, c).start()
    lax.fori_loop(0, min(WINDOW, steps), z_start, 0)

    gate_place, gate_weight = places(p % 2)
    row_at = lax.broadcasted_iota(jnp.int32, (group, 8 * CAP, 128), 1)
    lane_at = lax.broadcasted_iota(jnp.int32, (group, 8 * CAP, 128), 2)
    ones = jnp.ones((count, 128), jnp.bfloat16)
    for start in range(0, experts, group):
        part = gate_weight[start:start + group]
        weighted = chosen_rows(gate_place, start) * jnp.broadcast_to(part[:, None, :], slot_of.shape)
        spread = jnp.dot(
            weighted.reshape(group * 8 * CAP, count).astype(jnp.bfloat16), ones, preferred_element_type=jnp.float32
        ).reshape(group, 8 * CAP, 128)
        line = jnp.sum(jnp.where(row_at == lane_at, spread, 0.0), axis=1, keepdims=True)
        gate_send[start:start + group] = line

    def g_copy(i, sign, core):
        expert = 2 * plane(i, sign) + core
        return remote(
            gate_send.at[expert], gate_recv.at[i], g_send.at[i, core], g_recv.at[i], expert, p, t
        )

    own_gate = local(gate_send.at[e], gate_recv.at[steps - 1], g_recv.at[steps - 1])

    def g_each(act):
        def g_step(i, carry):
            for core in range(2):
                @pl.when((c == 0) & (p // 2 == 1))
                def _():
                    act(g_copy(i, 1, core))

                @pl.when((c == 0) & (p // 2 == 0) & ((i != steps - 1) | (c != core)))
                def _():
                    act(g_copy(i, 0, core))
            return carry

        lax.fori_loop(0, steps, g_step, 0)

    g_each(lambda copy: copy.start())

    @pl.when((c == 0) & (p // 2 == 0))
    def _():
        own_gate.start()

    up_t, down_t, far_t = (t + 1) % 4, (t + 3) % 4, (t + 2) % 4

    def y_copy(i, sign, way, owner):
        return remote(
            arrived.at[i, owner, sign], arrived.at[i, owner, sign], y_send.at[i, sign, way], y_recv.at[i, sign, way],
            e, p, up_t if way == 0 else down_t,
        )

    def f_copy(i, way, owner):
        return remote(
            arrived.at[i, owner, way], arrived.at[i, owner, way], f_send.at[i, way], f_recv.at[i, way],
            e, p, up_t if way == 0 else down_t,
        )

    def far_copy(i):
        return remote(
            arrived.at[i, t, 1], arrived.at[i, t, 1], f_send.at[i, 1], f_recv.at[i, 1], e, p, far_t
        )

    def r_copy(i, k, owner):
        other = (p + k) % 4
        return remote(
            partial.at[i, other], sums.at[i, owner], r_send.at[i, k - 1], r_recv.at[i, k - 1], e, other, t
        )

    def r_part(i, k, index):
        other = (p + k) % 4
        return remote(
            partial.at[i, other, index], sums.at[i, p, index], r_send.at[i, k - 1], r_recv.at[i, k - 1], e, other, t
        )

    def take_z(i, sign):
        for core in range(2):
            z_copy(i, sign, core, core).wait_recv()
        y_copy(i, sign, 0, t).start()
        y_copy(i, sign, 1, t).start()
        if sign == 1:
            @pl.when(i == steps - 1)
            def _():
                far_copy(i).start()

    def take_y(i, sign):
        owner = down_t if sign == 0 else up_t
        y_copy(i, sign, sign, owner).wait_recv()
        if sign == 0:
            f_copy(i, sign, owner).start()
        else:
            @pl.when(i != steps - 1)
            def _():
                f_copy(i, sign, owner).start()

    def take_compact():
        for entry in OFFERS:
            @pl.when(t == entry[1])
            def _():
                offer(*entry).wait_recv()
        for taker in range(4):
            @pl.when(t == taker)
            def _():
                for unit in range(KEEP):
                    rank = (KEEP * taker + unit) // 4
                    at = (KEEP * taker + unit) * UNIT
                    value = offered[at:at + UNIT]
                    for holder in HOLDERS[rank]:
                        if holder != taker:
                            other = taken[(taker - holder) % 4 - 1, unit * UNIT:(unit + 1) * UNIT]
                            value = jnp.where(kept[rank] // 2 == holder, other, value)
                    compact[unit * UNIT:(unit + 1) * UNIT] = value

    def lhs(i, first, core):
        loaded = arrived[i, first:first + 2, :, core]
        return loaded.astype(jnp.float32).reshape(4 * 8 * CAP, lanes).astype(jnp.bfloat16)

    def multiply(i):
        f_copy(i, 0, far_t).wait_recv()
        f_copy(i, 1, far_t).wait_recv()
        y_copy(i, 0, 1, up_t).wait_recv()
        y_copy(i, 1, 0, down_t).wait_recv()
        low, high = lhs(i, 0, 0), lhs(i, 0, 1)
        grad_low, grad_high = lhs(i, 2, 0), lhs(i, 2, 1)

        def product(one, two, weight):
            return jnp.dot(one, weight[:lanes], preferred_element_type=jnp.float32) + jnp.dot(
                two, weight[lanes:], preferred_element_type=jnp.float32
            )

        for index, (one, two, weight) in enumerate(((low, high, wg), (low, high, wu), (grad_low, grad_high, wdt))):
            value = product(one, two, weight)
            for which in range(2):
                for sign in range(2):
                    at = (2 * which + sign) * 8 * CAP
                    partial[i, 2 * sign + which, index] = value[at:at + 8 * CAP]
            for k in range(1, 4):
                r_part(i, k, index).start()

    def finish(i):
        total = partial[i, p]
        for k in range(1, 4):
            r_copy(i, k, (p + 4 - k) % 4).wait_recv()
            total = total + sums[i, (p + 4 - k) % 4]
        hidden = total[0] / (1.0 + jnp.exp(-total[0])) * total[1]
        local(gate_send.at[e], gate_recv.at[i], g_recv.at[i]).wait()
        column = jnp.sum(
            jnp.where(row24 == lane24, jnp.broadcast_to(gate_recv[i], (8 * CAP, 128)), 0.0), axis=1, keepdims=True
        )
        acc[...] += column * hidden * total[2]

    for copy in copies[:2]:
        copy.wait()
    row24 = lax.broadcasted_iota(jnp.int32, (8 * CAP, 128), 0)
    lane24 = lax.broadcasted_iota(jnp.int32, (8 * CAP, 128), 1)
    acc[...] = jnp.zeros(acc.shape, jnp.float32)
    wdt[...] = jnp.transpose(wd[...].astype(jnp.float32)).astype(jnp.bfloat16)
    take_z(steps - 1, 0)

    def step(s, carry):
        @pl.when(s == 1)
        def _():
            take_y(steps - 1, 0)

        @pl.when((s >= 1) & (s < steps))
        def _():
            take_y(s - 1, 0)

        @pl.when((s >= 1) & (s < steps + 1))
        def _():
            take_y(s - 1, 1)

        @pl.when(s < steps - 1)
        def _():
            take_z(s, 0)

        @pl.when(s < steps)
        def _():
            take_z(s, 1)

        @pl.when(s < steps - WINDOW)
        def _():
            z_sent(s)
            z_start(s + WINDOW, 0)

        @pl.when((s >= 1) & (s < steps + 1))
        def _():
            multiply(s - 1)

        @pl.when(s >= 2)
        def _():
            finish(s - 2)

        @pl.when(s == steps // 2)
        def _():
            take_compact()
            local(compact, compact_out.at[0], local_sem.at[1]).start()
        return carry

    lax.fori_loop(0, steps + 2, step, 0)
    total = acc[...]
    share[...] = jnp.broadcast_to(jnp.sum(total, axis=0, keepdims=True), share.shape)
    shares[p] = share[...]

    def s_copy(k, owner):
        return remote(share, shares.at[owner], s_send.at[k - 1], s_recv.at[k - 1], e, (p + k) % 4, t)

    for k in range(1, 4):
        s_copy(k, p).start()
    for k in range(1, 4):
        s_copy(k, (p + 4 - k) % 4).wait_recv()
    out[0] = jnp.abs(shares[0] + shares[2])
    out[1] = jnp.abs(shares[1] + shares[3])

    for k in range(1, 4):
        s_copy(k, p).wait_send()
    for k in range(1, 8):
        info_copy(k, (b + k) % 8, b).wait_send()
        raw_copy(k, (b + k) % 8, b).wait_send()
    g_each(lambda copy: copy.wait_send())

    each_offer(lambda copy: copy.wait_send())
    local(compact, compact_out.at[0], local_sem.at[1]).wait()

    def drain(i, carry):
        @pl.when(i >= steps - WINDOW)
        def _():
            z_sent(i)

        for way in range(2):
            for sign in range(2):
                y_copy(i, sign, way, t).wait_send()
            f_copy(i, way, down_t if way == 0 else up_t).wait_send()
        for k in range(1, 4):
            r_copy(i, k, p).wait_send()
        return carry

    lax.fori_loop(0, steps, drain, 0)


def routed(tokens, cotangent, routes, route_gate, dropped, gate_weight, up_weight, down_weight, experts):
    steps = experts // 4
    rows, width = tokens.shape[1:]
    lanes = width // 8
    depth, columns = gate_weight.shape[1:]
    slab = CAP
    anywhere = pl.BlockSpec(memory_space=pltpu.HBM)
    vmem = pl.BlockSpec(memory_space=pltpu.VMEM)
    half, full, dma = jnp.bfloat16, jnp.float32, pltpu.SemaphoreType.DMA
    return pl.pallas_call(
        functools.partial(kernel, experts),
        out_shape=(
            jax.ShapeDtypeStruct((2, 1, columns), full),
            jax.ShapeDtypeStruct((1, KEEP * UNIT, depth), half),
        ),
        in_specs=[anywhere] * 4 + [pl.BlockSpec(memory_space=pltpu.SMEM)] + [anywhere] * 3,
        out_specs=(vmem, anywhere),
        scratch_shapes=[
            pltpu.VMEM((rows, width), half),
            pltpu.VMEM((2, 2, rows), jnp.int32),
            pltpu.VMEM((2, 2, rows), half),
            pltpu.VMEM((8, rows, lanes), half),
            pltpu.VMEM((2, 8, 128), full),
            pltpu.VMEM((8, 2, 8, 128), full),
            pltpu.VMEM((experts * slab, 8, lanes), half),
            pltpu.VMEM((experts, 1, 128), full),
            pltpu.VMEM((steps, 1, 128), full),
            pltpu.VMEM((steps, 4, 2, 2, slab, 8, lanes), half),
            pltpu.VMEM((depth, columns), half),
            pltpu.VMEM((depth, columns), half),
            pltpu.VMEM((columns, depth), half),
            pltpu.VMEM((depth, columns), half),
            pltpu.VMEM((steps, 4, 3, 8 * CAP, columns), full),
            pltpu.VMEM((steps, 4, 3, 8 * CAP, columns), full),
            pltpu.VMEM((8 * CAP, columns), full),
            pltpu.VMEM((1, columns), full),
            pltpu.VMEM((4, 1, columns), full),
            pltpu.VMEM((KEEP * BLOCK, depth), half),
            pltpu.VMEM((3, KEEP * UNIT, depth), half),
            pltpu.VMEM((KEEP * UNIT, depth), half),
            dma((7,)),
            dma((8,)), dma((8,)), dma((8,)), dma((8,)),
            dma((steps, 2, 2)), dma((steps, 2, 2)),
            dma((steps, 2)), dma((steps,)),
            dma((steps, 2, 2)), dma((steps, 2, 2)), dma((steps, 2)), dma((steps, 2)),
            dma((steps, 3)), dma((steps, 3)), dma((3,)), dma((3,)), dma((3,)), dma((3,)),
        ],
        compiler_params=pltpu.CompilerParams(
            collective_id=0, has_side_effects=True, vmem_limit_bytes=62 * 1024 * 1024
        ),
        cost_estimate=pl.CostEstimate(flops=4 * 10**9, transcendentals=10**5, bytes_accessed=2 * 10**8),
    )(tokens, cotangent, routes, route_gate, dropped, gate_weight, up_weight, down_weight)


def body(tokens, cotangent, route_gate, routes, gate_weight, up_weight, down_weight, dropped):
    return routed(
        tokens, cotangent, jnp.transpose(routes, (0, 2, 1)), jnp.transpose(route_gate, (0, 2, 1)), dropped,
        gate_weight, up_weight, down_weight, lax.axis_size("expert"),
    )


def solution(mesh):
    return jax.shard_map(
        body,
        mesh=mesh,
        in_specs=(
            P(None, ("expert", "dp"), None),
            P(None, ("expert", "dp"), None),
            P(None, ("expert", "dp"), None),
            P(None, ("expert", "dp"), None),
            P("expert", "dp", "tensor"),
            P("expert", "dp", "tensor"),
            P("expert", "tensor", "dp"),
            P("expert", None),
        ),
        out_specs=(P(None, "expert", "tensor"), P("expert", "tensor", "dp")),
        check_vma=False,
    )
```

```python
import functools

import jax
import jax.numpy as jnp
from jax import lax
from jax.experimental import pallas as pl
from jax.experimental.pallas import tpu as pltpu
from jax.sharding import PartitionSpec as P

BLOCK = 128
KEEP = 5
CAP = 3
MESH = pl.DeviceIdType.MESH
UNIT = 32
WINDOW = 4
AHEAD = 384
OFFERS = ((0, 1, 5, 3), (1, 0, 0, 5), (1, 2, 10, 5), (1, 3, 15, 1), (2, 0, 4, 1), (2, 1, 5, 5), (2, 3, 15, 5), (3, 2, 12, 3))
HOLDERS = ((0, 1), (0, 1, 2), (1, 2), (1, 2, 3), (2, 3))


def kernel(
    experts,
    tokens, cotangent, routes, route_gate, dropped_in, gate_w, up_w, down_w,
    out, compact_out,
    mine, own_routes, own_gates, dropped, raw, info_own, info_all, packed, gate_send, gate_recv, arrived, wg, wu, wd, wdt, partial, sums, acc, share, shares, offered, taken, compact,
    local_sem, raw_send, raw_recv, info_send, info_recv, z_send, z_recv, g_send, g_recv,
    y_send, y_recv, f_send, f_recv, r_send, r_recv, s_send, s_recv, c_send, c_recv,
):
    planes = experts // 2
    steps = planes // 2
    rows = tokens.shape[1]
    width = tokens.shape[2]
    lanes = width // 8
    slab = 8 * CAP // 8
    e = lax.axis_index("expert")
    p = lax.axis_index("dp")
    t = lax.axis_index("tensor")
    z = e // 2
    c = e % 2
    b = 2 * p + c

    def local(src, dst, sem):
        return pltpu.make_async_copy(src, dst, sem)

    def remote(src, dst, send, recv, expert, dp, tensor):
        return pltpu.make_async_remote_copy(
            src_ref=src, dst_ref=dst, send_sem=send, recv_sem=recv,
            device_id={"expert": expert, "dp": dp, "tensor": tensor}, device_id_type=MESH,
        )

    barrier = pltpu.get_barrier_semaphore()

    def greet(expert, dp, tensor):
        pl.semaphore_signal(
            barrier, inc=1, device_id={"expert": expert, "dp": dp, "tensor": tensor}, device_id_type=MESH
        )

    def greet_z(k, carry):
        greet((e + k) % experts, p, t)
        return carry

    lax.fori_loop(1, experts, greet_z, 0)
    for k in range(1, 4):
        greet(e, (p + k) % 4, t)
        greet(2 * z + 1 - c, (p + k) % 4, t)
        greet(e, p, (t + k) % 4)

    for index in range(4):
        source = tokens if index < 2 else cotangent

        @pl.when(t == index)
        def _():
            local(source.at[index % 2], mine, local_sem.at[0]).start()

    copies = [local(gate_w.at[0], wg, local_sem.at[1]), local(up_w.at[0], wu, local_sem.at[2]),
              local(down_w.at[0], wd, local_sem.at[3])]
    small = [local(routes, own_routes, local_sem.at[5]), local(route_gate, own_gates, local_sem.at[6])]
    for copy in small:
        copy.start()
    local(dropped_in, dropped, local_sem.at[7]).start()
    for copy in copies:
        copy.start()

    for copy in small:
        copy.wait()
    lane = lax.broadcasted_iota(jnp.int32, (2, 128), 1)
    own_lanes = lane // rows == b % 4
    spread_of = jnp.where(
        lax.broadcasted_iota(jnp.int32, (rows, 128), 0) == lax.broadcasted_iota(jnp.int32, (rows, 128), 1) % rows, 1.0, 0.0
    ).astype(jnp.bfloat16)
    info_own[...] = jnp.zeros(info_own.shape, jnp.float32)
    for which in range(2):
        for at, lines in ((0, own_routes[which].astype(jnp.float32)), (2, own_gates[which].astype(jnp.float32))):
            wide = jnp.dot(lines.astype(jnp.bfloat16), spread_of, preferred_element_type=jnp.float32)
            info_own[which, at:at + 2] = jnp.where(own_lanes, wide, 0.0)
    info_all[b] = info_own[...]
    local(tokens.at[0], mine, local_sem.at[0]).wait()
    pl.semaphore_wait(barrier, experts - 1 + 9)

    parts = ((0, AHEAD), (AHEAD, lanes - AHEAD))

    def raw_copy(part, k, other, owner):
        start, size = parts[part]
        return remote(
            mine.at[:, pl.ds(pl.multiple_of(other * lanes + start, 128), size)], raw.at[owner, :, pl.ds(start, size)],
            raw_send.at[part, k], raw_recv.at[part, k], 2 * z + other % 2, other // 2, t,
        )

    def info_copy(k, other, owner):
        return remote(
            info_own, info_all.at[owner], info_send.at[k], info_recv.at[k], 2 * z + other % 2, other // 2, t
        )

    own_raw = local(mine.at[:, pl.ds(pl.multiple_of(b * lanes, 128), lanes)], raw.at[b], local_sem.at[4])
    own_raw.start()
    for k in range(1, 8):
        info_copy(k, (b + k) % 8, b).start()
    for k in range(1, 8):
        raw_copy(0, k, (b + k) % 8, b).start()

    local(dropped_in, dropped, local_sem.at[7]).wait()
    first, second, third = dropped[0, 0], dropped[0, 1], dropped[0, 2]
    least = jnp.minimum(first, jnp.minimum(second, third))
    most = jnp.maximum(first, jnp.maximum(second, third))
    middle = first + second + third - least - most
    kept = []
    for rank in range(KEEP):
        number = jnp.where(least <= rank, rank + 1, rank)
        number = jnp.where(middle <= number, number + 1, number)
        kept.append(jnp.where(most <= number, number + 1, number))
    copies[2].wait()
    for rank in range(KEEP):
        offered[rank * BLOCK:(rank + 1) * BLOCK] = jnp.where(kept[rank] == 2 * t, wd[:BLOCK], wd[BLOCK:])

    def offer(holder, taker, start, size):
        away = (taker - holder) % 4 - 1
        return remote(
            offered.at[pl.ds(start * UNIT, size * UNIT)], taken.at[away, pl.ds((start - KEEP * taker) * UNIT, size * UNIT)],
            c_send.at[away], c_recv.at[away], e, p, taker,
        )

    def each_offer(act):
        for entry in OFFERS:
            @pl.when(t == entry[0])
            def _():
                act(offer(*entry))

    each_offer(lambda copy: copy.start())
    for k in range(1, 8):
        raw_copy(1, k, (b + k) % 8, b).start()
    for k in range(1, 8):
        info_copy(k, (b + k) % 8, (b + 8 - k) % 8).wait_recv()

    count = 8 * rows

    def places(which):
        low = info_all[0, which] + info_all[1, which] + info_all[2, which] + info_all[3, which]
        high = info_all[4, which] + info_all[5, which] + info_all[6, which] + info_all[7, which]
        both = jnp.concatenate([low, high], axis=1)
        expert_of = lax.broadcasted_iota(jnp.int32, (experts, count), 0).astype(jnp.float32)
        first = jnp.broadcast_to(both[0:1], (experts, count)) == expert_of
        second = jnp.broadcast_to(both[1:2], (experts, count)) == expert_of
        chosen = jnp.where(first | second, 1.0, 0.0)
        above = lax.broadcasted_iota(jnp.int32, (count, count), 0)
        across = lax.broadcasted_iota(jnp.int32, (count, count), 1)
        before = jnp.where((above < across) & (above // rows == across // rows), 1.0, 0.0)
        rank = jnp.dot(
            chosen.astype(jnp.bfloat16), before.astype(jnp.bfloat16), preferred_element_type=jnp.float32
        )
        block_of = lax.broadcasted_iota(jnp.int32, (experts, count), 1) // rows
        place = jnp.where(chosen > 0.0, rank + CAP * block_of.astype(jnp.float32), -1.0)
        weight = jnp.where(first, jnp.broadcast_to(both[2:3], (experts, count)), 0.0) + jnp.where(
            second, jnp.broadcast_to(both[3:4], (experts, count)), 0.0
        )
        return place, weight

    group = 8
    slot_of = lax.broadcasted_iota(jnp.int32, (group, 8 * CAP, count), 1).astype(jnp.float32)

    def chosen_rows(place, start):
        part = place[start:start + group]
        return jnp.where(jnp.broadcast_to(part[:, None, :], slot_of.shape) == slot_of, 1.0, 0.0)

    place, _ = places(t % 2)
    own_raw.wait()

    def pack(part):
        start, size = parts[part]
        for k in range(1, 8):
            raw_copy(part, k, (b + k) % 8, (b + 8 - k) % 8).wait_recv()
        whole = raw[:, :, start:start + size].reshape(count, size)
        for first_expert in range(0, experts, group):
            select = chosen_rows(place, first_expert).reshape(group * 8 * CAP, count).astype(jnp.bfloat16)
            values = jnp.dot(select, whole, preferred_element_type=jnp.float32)
            packed[slab * first_expert:slab * (first_expert + group), :, start:start + size] = values.reshape(
                slab * group, 8, size
            ).astype(jnp.bfloat16)

    def plane(i, sign):
        return (z + (i + 1 if sign else planes - (i + 1) % steps)) % planes

    def z_copy(i, sign, core, owner_core):
        expert = 2 * plane(i, sign) + core
        return remote(
            packed.at[pl.ds(expert * slab, slab)], arrived.at[i, t, sign, owner_core],
            z_send.at[i, sign, core], z_recv.at[i, sign, owner_core], expert, p, t,
        )

    def z_part(i, sign, core, part):
        expert = 2 * plane(i, sign) + core
        span = pl.ds(*parts[part])
        return remote(
            packed.at[pl.ds(expert * slab, slab), :, span], arrived.at[i, t, sign, c, :, :, span],
            z_send.at[i, sign, core], z_recv.at[i, sign, c], expert, p, t,
        )

    def z_start(i, carry):
        for core in range(2):
            z_copy(i, 1, core, c).start()

            @pl.when(i != steps - 1)
            def _():
                z_copy(i, 0, core, c).start()
        return carry

    window = min(WINDOW, steps - 1)
    for part in range(2):
        pack(part)

        def z_begin(i, carry):
            for core in range(2):
                for sign in (1, 0):
                    z_part(i, sign, core, part).start()
            return carry

        lax.fori_loop(0, window, z_begin, 0)

    def z_sent(i):
        for sign in range(2):
            for core in range(2):
                if sign == 1:
                    z_copy(i, 1, core, c).wait_send()
                else:
                    @pl.when((i != steps - 1) | (c != core))
                    def _():
                        z_copy(i, 0, core, c).wait_send()

    own_slab = local(packed.at[pl.ds(e * slab, slab)], arrived.at[steps - 1, t, 0, c], z_recv.at[steps - 1, 0, c])
    own_slab.start()
    for core in range(2):
        @pl.when(c != core)
        def _():
            z_copy(steps - 1, 0, core, c).start()

    gate_place, gate_weight = places(p % 2)
    row_at = lax.broadcasted_iota(jnp.int32, (group, 8 * CAP, 128), 1)
    lane_at = lax.broadcasted_iota(jnp.int32, (group, 8 * CAP, 128), 2)
    ones = jnp.ones((count, 128), jnp.bfloat16)
    for start in range(0, experts, group):
        part = gate_weight[start:start + group]
        weighted = chosen_rows(gate_place, start) * jnp.broadcast_to(part[:, None, :], slot_of.shape)
        spread = jnp.dot(
            weighted.reshape(group * 8 * CAP, count).astype(jnp.bfloat16), ones, preferred_element_type=jnp.float32
        ).reshape(group, 8 * CAP, 128)
        line = jnp.sum(jnp.where(row_at == lane_at, spread, 0.0), axis=1, keepdims=True)
        gate_send[start:start + group] = line

    def g_copy(i, sign, core):
        expert = 2 * plane(i, sign) + core
        return remote(
            gate_send.at[expert], gate_recv.at[i], g_send.at[i, core], g_recv.at[i], expert, p, t
        )

    own_gate = local(gate_send.at[e], gate_recv.at[steps - 1], g_recv.at[steps - 1])

    def g_each(act):
        def g_step(i, carry):
            for core in range(2):
                @pl.when((c == 0) & (p // 2 == 1))
                def _():
                    act(g_copy(i, 1, core))

                @pl.when((c == 0) & (p // 2 == 0) & ((i != steps - 1) | (c != core)))
                def _():
                    act(g_copy(i, 0, core))
            return carry

        lax.fori_loop(0, steps, g_step, 0)

    g_each(lambda copy: copy.start())

    @pl.when((c == 0) & (p // 2 == 0))
    def _():
        own_gate.start()

    up_t, down_t, far_t = (t + 1) % 4, (t + 3) % 4, (t + 2) % 4

    def y_copy(i, sign, way, owner):
        return remote(
            arrived.at[i, owner, sign], arrived.at[i, owner, sign], y_send.at[i, sign, way], y_recv.at[i, sign, way],
            e, p, up_t if way == 0 else down_t,
        )

    def f_copy(i, way, owner):
        return remote(
            arrived.at[i, owner, way], arrived.at[i, owner, way], f_send.at[i, way], f_recv.at[i, way],
            e, p, up_t if way == 0 else down_t,
        )

    def far_copy(i):
        return remote(
            arrived.at[i, t, 1], arrived.at[i, t, 1], f_send.at[i, 1], f_recv.at[i, 1], e, p, far_t
        )

    def r_copy(i, k, owner):
        other = (p + k) % 4
        return remote(
            partial.at[i, other], sums.at[i, owner], r_send.at[i, k - 1], r_recv.at[i, k - 1], e, other, t
        )

    def r_part(i, k, index):
        other = (p + k) % 4
        return remote(
            partial.at[i, other, index], sums.at[i, p, index], r_send.at[i, k - 1], r_recv.at[i, k - 1], e, other, t
        )

    def take_z(i, sign):
        for core in range(2):
            z_copy(i, sign, core, core).wait_recv()
        y_copy(i, sign, 0, t).start()
        y_copy(i, sign, 1, t).start()
        if sign == 1:
            @pl.when(i == steps - 1)
            def _():
                far_copy(i).start()

    def take_y(i, sign):
        owner = down_t if sign == 0 else up_t
        y_copy(i, sign, sign, owner).wait_recv()
        if sign == 0:
            f_copy(i, sign, owner).start()
        else:
            @pl.when(i != steps - 1)
            def _():
                f_copy(i, sign, owner).start()

    def take_compact():
        for entry in OFFERS:
            @pl.when(t == entry[1])
            def _():
                offer(*entry).wait_recv()
        for taker in range(4):
            @pl.when(t == taker)
            def _():
                for unit in range(KEEP):
                    rank = (KEEP * taker + unit) // 4
                    at = (KEEP * taker + unit) * UNIT
                    value = offered[at:at + UNIT]
                    for holder in HOLDERS[rank]:
                        if holder != taker:
                            other = taken[(taker - holder) % 4 - 1, unit * UNIT:(unit + 1) * UNIT]
                            value = jnp.where(kept[rank] // 2 == holder, other, value)
                    compact[unit * UNIT:(unit + 1) * UNIT] = value

    def lhs(i, first, core):
        loaded = arrived[i, first:first + 2, :, core]
        return loaded.astype(jnp.float32).reshape(4 * 8 * CAP, lanes).astype(jnp.bfloat16)

    def multiply(i):
        f_copy(i, 0, far_t).wait_recv()
        f_copy(i, 1, far_t).wait_recv()
        y_copy(i, 0, 1, up_t).wait_recv()
        y_copy(i, 1, 0, down_t).wait_recv()
        low, high = lhs(i, 0, 0), lhs(i, 0, 1)
        grad_low, grad_high = lhs(i, 2, 0), lhs(i, 2, 1)

        def product(one, two, weight):
            return jnp.dot(one, weight[:lanes], preferred_element_type=jnp.float32) + jnp.dot(
                two, weight[lanes:], preferred_element_type=jnp.float32
            )

        for index, (one, two, weight) in enumerate(((low, high, wg), (low, high, wu), (grad_low, grad_high, wdt))):
            value = product(one, two, weight)
            for which in range(2):
                for sign in range(2):
                    at = (2 * which + sign) * 8 * CAP
                    partial[i, 2 * sign + which, index] = value[at:at + 8 * CAP]
            for k in range(1, 4):
                r_part(i, k, index).start()

    def finish(i):
        total = partial[i, p]
        for k in range(1, 4):
            r_copy(i, k, (p + 4 - k) % 4).wait_recv()
            total = total + sums[i, (p + 4 - k) % 4]
        hidden = total[0] / (1.0 + jnp.exp(-total[0])) * total[1]
        local(gate_send.at[e], gate_recv.at[i], g_recv.at[i]).wait()
        column = jnp.sum(
            jnp.where(row24 == lane24, jnp.broadcast_to(gate_recv[i], (8 * CAP, 128)), 0.0), axis=1, keepdims=True
        )
        acc[...] += column * hidden * total[2]

    for copy in copies[:2]:
        copy.wait()
    row24 = lax.broadcasted_iota(jnp.int32, (8 * CAP, 128), 0)
    lane24 = lax.broadcasted_iota(jnp.int32, (8 * CAP, 128), 1)
    acc[...] = jnp.zeros(acc.shape, jnp.float32)
    wdt[...] = jnp.transpose(wd[...].astype(jnp.float32)).astype(jnp.bfloat16)
    take_z(steps - 1, 0)

    def step(s, carry):
        @pl.when(s == 1)
        def _():
            take_y(steps - 1, 0)

        @pl.when((s >= 1) & (s < steps))
        def _():
            take_y(s - 1, 0)

        @pl.when((s >= 1) & (s < steps + 1))
        def _():
            take_y(s - 1, 1)

        @pl.when(s < steps - 1)
        def _():
            take_z(s, 0)

        @pl.when(s < steps)
        def _():
            take_z(s, 1)

        @pl.when(s < steps - window)
        def _():
            z_sent(s)
            z_start(s + window, 0)

        @pl.when((s >= 1) & (s < steps + 1))
        def _():
            multiply(s - 1)

        @pl.when(s >= 2)
        def _():
            finish(s - 2)

        @pl.when(s == steps // 2)
        def _():
            take_compact()
            local(compact, compact_out.at[0], local_sem.at[1]).start()
        return carry

    lax.fori_loop(0, steps + 2, step, 0)
    total = acc[...]
    share[...] = jnp.broadcast_to(jnp.sum(total, axis=0, keepdims=True), share.shape)
    shares[p] = share[...]

    def s_copy(k, owner):
        return remote(share, shares.at[owner], s_send.at[k - 1], s_recv.at[k - 1], e, (p + k) % 4, t)

    for k in range(1, 4):
        s_copy(k, p).start()
    for k in range(1, 4):
        s_copy(k, (p + 4 - k) % 4).wait_recv()
    out[0] = jnp.abs(shares[0] + shares[2])
    out[1] = jnp.abs(shares[1] + shares[3])

    for k in range(1, 4):
        s_copy(k, p).wait_send()
    for k in range(1, 8):
        info_copy(k, (b + k) % 8, b).wait_send()
        for part in range(2):
            raw_copy(part, k, (b + k) % 8, b).wait_send()
    g_each(lambda copy: copy.wait_send())

    each_offer(lambda copy: copy.wait_send())
    local(compact, compact_out.at[0], local_sem.at[1]).wait()

    def drain(i, carry):
        @pl.when(i >= steps - window)
        def _():
            z_sent(i)

        for way in range(2):
            for sign in range(2):
                y_copy(i, sign, way, t).wait_send()
            f_copy(i, way, down_t if way == 0 else up_t).wait_send()
        for k in range(1, 4):
            r_copy(i, k, p).wait_send()
        return carry

    lax.fori_loop(0, steps, drain, 0)


def routed(tokens, cotangent, routes, route_gate, dropped, gate_weight, up_weight, down_weight, experts):
    steps = experts // 4
    rows, width = tokens.shape[1:]
    lanes = width // 8
    depth, columns = gate_weight.shape[1:]
    slab = CAP
    anywhere = pl.BlockSpec(memory_space=pltpu.HBM)
    vmem = pl.BlockSpec(memory_space=pltpu.VMEM)
    half, full, dma = jnp.bfloat16, jnp.float32, pltpu.SemaphoreType.DMA
    return pl.pallas_call(
        functools.partial(kernel, experts),
        out_shape=(
            jax.ShapeDtypeStruct((2, 1, columns), full),
            jax.ShapeDtypeStruct((1, KEEP * UNIT, depth), half),
        ),
        in_specs=[anywhere] * 8,
        out_specs=(vmem, anywhere),
        scratch_shapes=[
            pltpu.VMEM((rows, width), half),
            pltpu.VMEM((2, 2, rows), jnp.int32),
            pltpu.VMEM((2, 2, rows), half),
            pltpu.SMEM((1, 3), jnp.int32),
            pltpu.VMEM((8, rows, lanes), half),
            pltpu.VMEM((2, 8, 128), full),
            pltpu.VMEM((8, 2, 8, 128), full),
            pltpu.VMEM((experts * slab, 8, lanes), half),
            pltpu.VMEM((experts, 1, 128), full),
            pltpu.VMEM((steps, 1, 128), full),
            pltpu.VMEM((steps, 4, 2, 2, slab, 8, lanes), half),
            pltpu.VMEM((depth, columns), half),
            pltpu.VMEM((depth, columns), half),
            pltpu.VMEM((columns, depth), half),
            pltpu.VMEM((depth, columns), half),
            pltpu.VMEM((steps, 4, 3, 8 * CAP, columns), full),
            pltpu.VMEM((steps, 4, 3, 8 * CAP, columns), full),
            pltpu.VMEM((8 * CAP, columns), full),
            pltpu.VMEM((1, columns), full),
            pltpu.VMEM((4, 1, columns), full),
            pltpu.VMEM((KEEP * BLOCK, depth), half),
            pltpu.VMEM((3, KEEP * UNIT, depth), half),
            pltpu.VMEM((KEEP * UNIT, depth), half),
            dma((8,)),
            dma((2, 8)), dma((2, 8)), dma((8,)), dma((8,)),
            dma((steps, 2, 2)), dma((steps, 2, 2)),
            dma((steps, 2)), dma((steps,)),
            dma((steps, 2, 2)), dma((steps, 2, 2)), dma((steps, 2)), dma((steps, 2)),
            dma((steps, 3)), dma((steps, 3)), dma((3,)), dma((3,)), dma((3,)), dma((3,)),
        ],
        compiler_params=pltpu.CompilerParams(
            collective_id=0, has_side_effects=True, vmem_limit_bytes=62 * 1024 * 1024
        ),
        cost_estimate=pl.CostEstimate(flops=4 * 10**9, transcendentals=10**5, bytes_accessed=2 * 10**8),
    )(tokens, cotangent, routes, route_gate, dropped, gate_weight, up_weight, down_weight)


def body(tokens, cotangent, route_gate, routes, gate_weight, up_weight, down_weight, dropped):
    return routed(
        tokens, cotangent, jnp.transpose(routes, (0, 2, 1)), jnp.transpose(route_gate, (0, 2, 1)), dropped,
        gate_weight, up_weight, down_weight, lax.axis_size("expert"),
    )


def solution(mesh):
    return jax.shard_map(
        body,
        mesh=mesh,
        in_specs=(
            P(None, ("expert", "dp"), None),
            P(None, ("expert", "dp"), None),
            P(None, ("expert", "dp"), None),
            P(None, ("expert", "dp"), None),
            P("expert", "dp", "tensor"),
            P("expert", "dp", "tensor"),
            P("expert", "tensor", "dp"),
            P("expert", None),
        ),
        out_specs=(P(None, "expert", "tensor"), P("expert", "tensor", "dp")),
        check_vma=False,
    )
```

```python
import functools

import jax
import jax.numpy as jnp
from jax import lax
from jax.experimental import pallas as pl
from jax.experimental.pallas import tpu as pltpu
from jax.sharding import PartitionSpec as P

BLOCK = 128
KEEP = 5
CAP = 3
MESH = pl.DeviceIdType.MESH
UNIT = 32
WINDOW = 4
AHEAD = 384
OFFERS = ((0, 1, 5, 3), (1, 0, 0, 5), (1, 2, 10, 5), (1, 3, 15, 1), (2, 0, 4, 1), (2, 1, 5, 5), (2, 3, 15, 5), (3, 2, 12, 3))
HOLDERS = ((0, 1), (0, 1, 2), (1, 2), (1, 2, 3), (2, 3))


def kernel(
    experts,
    tokens, cotangent, routes, route_gate, dropped_in, gate_w, up_w, down_w,
    out, compact_out,
    mine, own_routes, own_gates, dropped, raw, info_own, info_all, packed, gate_send, gate_recv, arrived, wg, wu, wd, wdt, partial, sums, acc, last_part, last_sums, gate_last, share, shares, offered, taken, compact,
    local_sem, raw_send, raw_recv, info_send, info_recv, z_send, z_recv, g_send, g_recv,
    y_send, y_recv, f_send, f_recv, r_send, r_recv, s_send, s_recv, c_send, c_recv, l_send, l_recv, gl_send, gl_recv,
):
    planes = experts // 2
    steps = planes // 2
    rows = tokens.shape[1]
    width = tokens.shape[2]
    lanes = width // 8
    slab = 8 * CAP // 8
    e = lax.axis_index("expert")
    p = lax.axis_index("dp")
    t = lax.axis_index("tensor")
    z = e // 2
    c = e % 2
    b = 2 * p + c

    def local(src, dst, sem):
        return pltpu.make_async_copy(src, dst, sem)

    def remote(src, dst, send, recv, expert, dp, tensor):
        return pltpu.make_async_remote_copy(
            src_ref=src, dst_ref=dst, send_sem=send, recv_sem=recv,
            device_id={"expert": expert, "dp": dp, "tensor": tensor}, device_id_type=MESH,
        )

    barrier = pltpu.get_barrier_semaphore()

    def greet(expert, dp, tensor):
        pl.semaphore_signal(
            barrier, inc=1, device_id={"expert": expert, "dp": dp, "tensor": tensor}, device_id_type=MESH
        )

    def greet_z(k, carry):
        greet((e + k) % experts, p, t)
        return carry

    lax.fori_loop(1, experts, greet_z, 0)
    for k in range(1, 4):
        greet(e, (p + k) % 4, t)
        greet(2 * z + 1 - c, (p + k) % 4, t)
        greet(e, p, (t + k) % 4)

    for index in range(4):
        source = tokens if index < 2 else cotangent

        @pl.when(t == index)
        def _():
            local(source.at[index % 2], mine, local_sem.at[0]).start()

    copies = [local(gate_w.at[0], wg, local_sem.at[1]), local(up_w.at[0], wu, local_sem.at[2]),
              local(down_w.at[0], wd, local_sem.at[3])]
    small = [local(routes, own_routes, local_sem.at[5]), local(route_gate, own_gates, local_sem.at[6])]
    for copy in small:
        copy.start()
    local(dropped_in, dropped, local_sem.at[7]).start()
    for copy in copies:
        copy.start()

    for copy in small:
        copy.wait()
    lane = lax.broadcasted_iota(jnp.int32, (2, 128), 1)
    own_lanes = lane // rows == b % 4
    spread_of = jnp.where(
        lax.broadcasted_iota(jnp.int32, (rows, 128), 0) == lax.broadcasted_iota(jnp.int32, (rows, 128), 1) % rows, 1.0, 0.0
    ).astype(jnp.bfloat16)
    info_own[...] = jnp.zeros(info_own.shape, jnp.float32)
    for which in range(2):
        for at, lines in ((0, own_routes[which].astype(jnp.float32)), (2, own_gates[which].astype(jnp.float32))):
            wide = jnp.dot(lines.astype(jnp.bfloat16), spread_of, preferred_element_type=jnp.float32)
            info_own[which, at:at + 2] = jnp.where(own_lanes, wide, 0.0)
    info_all[b] = info_own[...]
    local(tokens.at[0], mine, local_sem.at[0]).wait()
    pl.semaphore_wait(barrier, experts - 1 + 9)

    parts = ((0, AHEAD), (AHEAD, lanes - AHEAD))

    def raw_copy(part, k, other, owner):
        start, size = parts[part]
        return remote(
            mine.at[:, pl.ds(pl.multiple_of(other * lanes + start, 128), size)], raw.at[owner, :, pl.ds(start, size)],
            raw_send.at[part, k], raw_recv.at[part, k], 2 * z + other % 2, other // 2, t,
        )

    def info_copy(k, other, owner):
        return remote(
            info_own, info_all.at[owner], info_send.at[k], info_recv.at[k], 2 * z + other % 2, other // 2, t
        )

    own_raw = local(mine.at[:, pl.ds(pl.multiple_of(b * lanes, 128), lanes)], raw.at[b], local_sem.at[4])
    own_raw.start()
    for k in range(1, 8):
        info_copy(k, (b + k) % 8, b).start()
    for k in range(1, 8):
        raw_copy(0, k, (b + k) % 8, b).start()

    local(dropped_in, dropped, local_sem.at[7]).wait()
    first, second, third = dropped[0, 0], dropped[0, 1], dropped[0, 2]
    least = jnp.minimum(first, jnp.minimum(second, third))
    most = jnp.maximum(first, jnp.maximum(second, third))
    middle = first + second + third - least - most
    kept = []
    for rank in range(KEEP):
        number = jnp.where(least <= rank, rank + 1, rank)
        number = jnp.where(middle <= number, number + 1, number)
        kept.append(jnp.where(most <= number, number + 1, number))
    copies[2].wait()
    for rank in range(KEEP):
        offered[rank * BLOCK:(rank + 1) * BLOCK] = jnp.where(kept[rank] == 2 * t, wd[:BLOCK], wd[BLOCK:])

    def offer(holder, taker, start, size):
        away = (taker - holder) % 4 - 1
        return remote(
            offered.at[pl.ds(start * UNIT, size * UNIT)], taken.at[away, pl.ds((start - KEEP * taker) * UNIT, size * UNIT)],
            c_send.at[away], c_recv.at[away], e, p, taker,
        )

    def each_offer(act):
        for entry in OFFERS:
            @pl.when(t == entry[0])
            def _():
                act(offer(*entry))

    each_offer(lambda copy: copy.start())
    for k in range(1, 8):
        raw_copy(1, k, (b + k) % 8, b).start()
    for k in range(1, 8):
        info_copy(k, (b + k) % 8, (b + 8 - k) % 8).wait_recv()

    count = 8 * rows

    def places(which):
        low = info_all[0, which] + info_all[1, which] + info_all[2, which] + info_all[3, which]
        high = info_all[4, which] + info_all[5, which] + info_all[6, which] + info_all[7, which]
        both = jnp.concatenate([low, high], axis=1)
        expert_of = lax.broadcasted_iota(jnp.int32, (experts, count), 0).astype(jnp.float32)
        first = jnp.broadcast_to(both[0:1], (experts, count)) == expert_of
        second = jnp.broadcast_to(both[1:2], (experts, count)) == expert_of
        chosen = jnp.where(first | second, 1.0, 0.0)
        above = lax.broadcasted_iota(jnp.int32, (count, count), 0)
        across = lax.broadcasted_iota(jnp.int32, (count, count), 1)
        before = jnp.where((above < across) & (above // rows == across // rows), 1.0, 0.0)
        rank = jnp.dot(
            chosen.astype(jnp.bfloat16), before.astype(jnp.bfloat16), preferred_element_type=jnp.float32
        )
        block_of = lax.broadcasted_iota(jnp.int32, (experts, count), 1) // rows
        place = jnp.where(chosen > 0.0, rank + CAP * block_of.astype(jnp.float32), -1.0)
        weight = jnp.where(first, jnp.broadcast_to(both[2:3], (experts, count)), 0.0) + jnp.where(
            second, jnp.broadcast_to(both[3:4], (experts, count)), 0.0
        )
        return place, weight

    group = 8
    slot_of = lax.broadcasted_iota(jnp.int32, (group, 8 * CAP, count), 1).astype(jnp.float32)

    def chosen_rows(place, start):
        part = place[start:start + group]
        return jnp.where(jnp.broadcast_to(part[:, None, :], slot_of.shape) == slot_of, 1.0, 0.0)

    place, _ = places(t % 2)
    own_raw.wait()

    def pack(part):
        start, size = parts[part]
        for k in range(1, 8):
            raw_copy(part, k, (b + k) % 8, (b + 8 - k) % 8).wait_recv()
        whole = raw[:, :, start:start + size].reshape(count, size)
        for first_expert in range(0, experts, group):
            select = chosen_rows(place, first_expert).reshape(group * 8 * CAP, count).astype(jnp.bfloat16)
            values = jnp.dot(select, whole, preferred_element_type=jnp.float32)
            packed[slab * first_expert:slab * (first_expert + group), :, start:start + size] = values.reshape(
                slab * group, 8, size
            ).astype(jnp.bfloat16)

    def plane(i, sign):
        return (z + (i + 1 if sign else planes - (i + 1) % steps)) % planes

    def z_copy(i, sign, core, owner_core):
        expert = 2 * plane(i, sign) + core
        return remote(
            packed.at[pl.ds(expert * slab, slab)], arrived.at[i, t, sign, owner_core],
            z_send.at[i, sign, core], z_recv.at[i, sign, owner_core], expert, p, t,
        )

    def z_part(i, sign, core, part):
        expert = 2 * plane(i, sign) + core
        span = pl.ds(*parts[part])
        return remote(
            packed.at[pl.ds(expert * slab, slab), :, span], arrived.at[i, t, sign, c, :, :, span],
            z_send.at[i, sign, core], z_recv.at[i, sign, c], expert, p, t,
        )

    def z_start(i, carry):
        for core in range(2):
            z_copy(i, 1, core, c).start()

            @pl.when(i != steps - 1)
            def _():
                z_copy(i, 0, core, c).start()
        return carry

    window = min(WINDOW, steps - 1)
    for part in range(2):
        pack(part)

        def z_begin(i, carry):
            for core in range(2):
                for sign in (1, 0):
                    z_part(i, sign, core, part).start()
            return carry

        lax.fori_loop(0, window, z_begin, 0)

    def z_sent(i):
        for sign in range(2):
            for core in range(2):
                if sign == 1:
                    z_copy(i, 1, core, c).wait_send()
                else:
                    @pl.when((i != steps - 1) | (c != core))
                    def _():
                        z_copy(i, 0, core, c).wait_send()

    own_slab = local(packed.at[pl.ds(e * slab, slab)], arrived.at[steps - 1, t, 0, c], z_recv.at[steps - 1, 0, c])
    own_slab.start()
    for core in range(2):
        @pl.when(c != core)
        def _():
            z_copy(steps - 1, 0, core, c).start()

    gate_place, gate_weight = places(p % 2)
    row_at = lax.broadcasted_iota(jnp.int32, (group, 8 * CAP, 128), 1)
    lane_at = lax.broadcasted_iota(jnp.int32, (group, 8 * CAP, 128), 2)
    ones = jnp.ones((count, 128), jnp.bfloat16)
    for start in range(0, experts, group):
        part = gate_weight[start:start + group]
        weighted = chosen_rows(gate_place, start) * jnp.broadcast_to(part[:, None, :], slot_of.shape)
        spread = jnp.dot(
            weighted.reshape(group * 8 * CAP, count).astype(jnp.bfloat16), ones, preferred_element_type=jnp.float32
        ).reshape(group, 8 * CAP, 128)
        line = jnp.sum(jnp.where(row_at == lane_at, spread, 0.0), axis=1, keepdims=True)
        gate_send[start:start + group] = line

    def g_copy(i, sign, core):
        expert = 2 * plane(i, sign) + core
        return remote(
            gate_send.at[expert], gate_recv.at[i], g_send.at[i, core], g_recv.at[i], expert, p, t
        )

    def far_gate(core):
        expert = 2 * plane(steps - 1, 1) + core
        return remote(gate_send.at[expert], gate_last, gl_send.at[core], gl_recv.at[0], expert, p, t)

    own_gate = local(gate_send.at[e], gate_recv.at[steps - 1], g_recv.at[steps - 1])

    def g_each(act):
        def g_step(i, carry):
            for core in range(2):
                @pl.when((c == 0) & (p // 2 == 1) & (i != steps - 1))
                def _():
                    act(g_copy(i, 1, core))

                @pl.when((c == 0) & (p // 2 == 0) & ((i != steps - 1) | (c != core)))
                def _():
                    act(g_copy(i, 0, core))
            return carry

        lax.fori_loop(0, steps, g_step, 0)
        for core in range(2):
            @pl.when(c == 0)
            def _():
                act(far_gate(core))

    g_each(lambda copy: copy.start())

    @pl.when((c == 0) & (p // 2 == 0))
    def _():
        own_gate.start()

    up_t, down_t, far_t = (t + 1) % 4, (t + 3) % 4, (t + 2) % 4

    def y_copy(i, sign, way, owner):
        return remote(
            arrived.at[i, owner, sign], arrived.at[i, owner, sign], y_send.at[i, sign, way], y_recv.at[i, sign, way],
            e, p, up_t if way == 0 else down_t,
        )

    def f_copy(i, way, owner):
        return remote(
            arrived.at[i, owner, way], arrived.at[i, owner, way], f_send.at[i, way], f_recv.at[i, way],
            e, p, up_t if way == 0 else down_t,
        )

    def far_copy(i):
        return remote(
            arrived.at[i, t, 1], arrived.at[i, t, 1], f_send.at[i, 1], f_recv.at[i, 1], e, p, far_t
        )

    def r_copy(i, k, owner):
        other = (p + k) % 4
        return remote(
            partial.at[i, other], sums.at[i, owner], r_send.at[i, k - 1], r_recv.at[i, k - 1], e, other, t
        )

    def r_part(i, k, index):
        other = (p + k) % 4
        return remote(
            partial.at[i, other, index], sums.at[i, p, index], r_send.at[i, k - 1], r_recv.at[i, k - 1], e, other, t
        )

    def take_z(i, sign):
        for core in range(2):
            z_copy(i, sign, core, core).wait_recv()
        y_copy(i, sign, 0, t).start()
        y_copy(i, sign, 1, t).start()
        if sign == 1:
            @pl.when(i == steps - 1)
            def _():
                far_copy(i).start()

    def take_y(i, sign):
        owner = down_t if sign == 0 else up_t
        y_copy(i, sign, sign, owner).wait_recv()
        if sign == 0:
            f_copy(i, sign, owner).start()
        else:
            @pl.when(i != steps - 1)
            def _():
                f_copy(i, sign, owner).start()

    def take_compact():
        for entry in OFFERS:
            @pl.when(t == entry[1])
            def _():
                offer(*entry).wait_recv()
        for taker in range(4):
            @pl.when(t == taker)
            def _():
                for unit in range(KEEP):
                    rank = (KEEP * taker + unit) // 4
                    at = (KEEP * taker + unit) * UNIT
                    value = offered[at:at + UNIT]
                    for holder in HOLDERS[rank]:
                        if holder != taker:
                            other = taken[(taker - holder) % 4 - 1, unit * UNIT:(unit + 1) * UNIT]
                            value = jnp.where(kept[rank] // 2 == holder, other, value)
                    compact[unit * UNIT:(unit + 1) * UNIT] = value

    def lhs(i, first, core):
        loaded = arrived[i, first:first + 2, :, core]
        return loaded.astype(jnp.float32).reshape(4 * 8 * CAP, lanes).astype(jnp.bfloat16)

    def product(one, two, weight):
        return jnp.dot(one, weight[:lanes], preferred_element_type=jnp.float32) + jnp.dot(
            two, weight[lanes:], preferred_element_type=jnp.float32
        )

    def multiply(i):
        f_copy(i, 0, far_t).wait_recv()
        f_copy(i, 1, far_t).wait_recv()
        y_copy(i, 0, 1, up_t).wait_recv()
        y_copy(i, 1, 0, down_t).wait_recv()
        low, high = lhs(i, 0, 0), lhs(i, 0, 1)
        grad_low, grad_high = lhs(i, 2, 0), lhs(i, 2, 1)
        for index, (one, two, weight) in enumerate(((low, high, wg), (low, high, wu), (grad_low, grad_high, wdt))):
            value = product(one, two, weight)
            for which in range(2):
                for sign in range(2):
                    at = (2 * which + sign) * 8 * CAP
                    partial[i, 2 * sign + which, index] = value[at:at + 8 * CAP]
            for k in range(1, 4):
                r_part(i, k, index).start()

    def last_copy(k, owner, index):
        other = (p + k) % 4
        if index is None:
            source, target = last_part.at[other], last_sums.at[owner]
        else:
            source, target = last_part.at[other, index], last_sums.at[owner, index]
        return remote(source, target, l_send.at[k - 1], l_recv.at[k - 1], e, other, t)

    def multiply_last(sign):
        i = steps - 1
        f_copy(i, sign, far_t).wait_recv()
        y_copy(i, sign, 1 - sign, down_t if sign else up_t).wait_recv()

        def rows_of(first, core):
            loaded = arrived[i, first:first + 2, sign, core]
            return loaded.astype(jnp.float32).reshape(2 * 8 * CAP, lanes).astype(jnp.bfloat16)

        low, high = rows_of(0, 0), rows_of(0, 1)
        grad_low, grad_high = rows_of(2, 0), rows_of(2, 1)
        middle = wg.shape[1] // 2
        for index, (one, two, weight) in enumerate(((low, high, wg), (low, high, wu), (grad_low, grad_high, wdt))):
            value = product(one, two, weight)
            for which in range(2):
                rows_at = value[which * 8 * CAP:(which + 1) * 8 * CAP]
                if sign == 0:
                    partial[i, which, index] = rows_at
                else:
                    last_part[which, index] = rows_at[:, :middle]
                    last_part[2 + which, index] = rows_at[:, middle:]
            for k in range(1, 4):
                if sign == 0:
                    @pl.when((p + k) % 4 < 2)
                    def _():
                        r_part(i, k, index).start()
                else:
                    last_copy(k, p, index).start()

    def finish(i):
        total = partial[i, p]
        for k in range(1, 4):
            r_copy(i, k, (p + 4 - k) % 4).wait_recv()
            total = total + sums[i, (p + 4 - k) % 4]
        local(gate_send.at[e], gate_recv.at[i], g_recv.at[i]).wait()
        acc[...] += gated(total, gate_recv[i])

    def gated(total, line):
        hidden = total[0] / (1.0 + jnp.exp(-total[0])) * total[1]
        column = jnp.sum(
            jnp.where(row24 == lane24, jnp.broadcast_to(line, (8 * CAP, 128)), 0.0), axis=1, keepdims=True
        )
        return column * hidden * total[2]

    def finish_last():
        total = last_part[p]
        for k in range(1, 4):
            last_copy(k, (p + 4 - k) % 4, None).wait_recv()
            total = total + last_sums[(p + 4 - k) % 4]
        local(gate_send.at[e], gate_last, gl_recv.at[0]).wait()
        value = gated(total, gate_last[...])
        middle = wg.shape[1] // 2

        @pl.when(p // 2 == 0)
        def _():
            acc[:, :middle] += value

        @pl.when(p // 2 == 1)
        def _():
            acc[:, middle:] += value

    for copy in copies[:2]:
        copy.wait()
    row24 = lax.broadcasted_iota(jnp.int32, (8 * CAP, 128), 0)
    lane24 = lax.broadcasted_iota(jnp.int32, (8 * CAP, 128), 1)
    acc[...] = jnp.zeros(acc.shape, jnp.float32)
    wdt[...] = jnp.transpose(wd[...].astype(jnp.float32)).astype(jnp.bfloat16)
    take_z(steps - 1, 0)

    def early():
        for k in range(1, 8):
            info_copy(k, (b + k) % 8, b).wait_send()
            for part in range(2):
                raw_copy(part, k, (b + k) % 8, b).wait_send()
        g_each(lambda copy: copy.wait_send())

    def drain(i, carry):
        @pl.when(i >= steps - window)
        def _():
            z_sent(i)

        for way in range(2):
            for sign in range(2):
                y_copy(i, sign, way, t).wait_send()
            f_copy(i, way, down_t if way == 0 else up_t).wait_send()
        for k in range(1, 4):
            @pl.when((i != steps - 1) | ((p + k) % 4 < 2))
            def _():
                r_copy(i, k, p).wait_send()
        return carry

    def step(s, carry):
        @pl.when(s == 1)
        def _():
            take_y(steps - 1, 0)

        @pl.when((s >= 1) & (s < steps))
        def _():
            take_y(s - 1, 0)

        @pl.when((s >= 1) & (s < steps + 1))
        def _():
            take_y(s - 1, 1)

        @pl.when(s < steps - 1)
        def _():
            take_z(s, 0)

        @pl.when(s < steps)
        def _():
            take_z(s, 1)

        @pl.when(s < steps - window)
        def _():
            z_sent(s)
            z_start(s + window, 0)

        @pl.when((s >= 1) & (s < steps))
        def _():
            multiply(s - 1)

        @pl.when(s == steps)
        def _():
            multiply_last(1)

        @pl.when((s >= 2) & (s < steps + 1))
        def _():
            finish(s - 2)

        @pl.when(s == 2)
        def _():
            early()

        @pl.when(s == 3)
        def _():
            multiply_last(0)

        @pl.when((s >= 4) & (s < steps + 1))
        def _():
            drain(s - 4, 0)

        @pl.when(s == 6)
        def _():
            each_offer(lambda copy: copy.wait_send())

        @pl.when((s == 5) & (p < 2))
        def _():
            finish(steps - 1)

        @pl.when(s == steps // 2)
        def _():
            take_compact()
            local(compact, compact_out.at[0], local_sem.at[1]).start()
        return carry

    lax.fori_loop(0, steps + 1, step, 0)
    finish_last()
    total = acc[...]
    share[...] = jnp.broadcast_to(jnp.sum(total, axis=0, keepdims=True), share.shape)
    shares[p] = share[...]

    def s_copy(k, owner):
        return remote(share, shares.at[owner], s_send.at[k - 1], s_recv.at[k - 1], e, (p + k) % 4, t)

    for k in range(1, 4):
        s_copy(k, p).start()
    for k in range(1, 4):
        last_copy(k, p, None).wait_send()
    local(compact, compact_out.at[0], local_sem.at[1]).wait()
    lax.fori_loop(steps - 3, steps, drain, 0)
    for k in range(1, 4):
        s_copy(k, (p + 4 - k) % 4).wait_recv()
    out[0] = jnp.abs(shares[0] + shares[2])
    out[1] = jnp.abs(shares[1] + shares[3])
    for k in range(1, 4):
        s_copy(k, p).wait_send()


def routed(tokens, cotangent, routes, route_gate, dropped, gate_weight, up_weight, down_weight, experts):
    steps = experts // 4
    rows, width = tokens.shape[1:]
    lanes = width // 8
    depth, columns = gate_weight.shape[1:]
    slab = CAP
    anywhere = pl.BlockSpec(memory_space=pltpu.HBM)
    vmem = pl.BlockSpec(memory_space=pltpu.VMEM)
    half, full, dma = jnp.bfloat16, jnp.float32, pltpu.SemaphoreType.DMA
    return pl.pallas_call(
        functools.partial(kernel, experts),
        out_shape=(
            jax.ShapeDtypeStruct((2, 1, columns), full),
            jax.ShapeDtypeStruct((1, KEEP * UNIT, depth), half),
        ),
        in_specs=[anywhere] * 8,
        out_specs=(vmem, anywhere),
        scratch_shapes=[
            pltpu.VMEM((rows, width), half),
            pltpu.VMEM((2, 2, rows), jnp.int32),
            pltpu.VMEM((2, 2, rows), half),
            pltpu.SMEM((1, 3), jnp.int32),
            pltpu.VMEM((8, rows, lanes), half),
            pltpu.VMEM((2, 8, 128), full),
            pltpu.VMEM((8, 2, 8, 128), full),
            pltpu.VMEM((experts * slab, 8, lanes), half),
            pltpu.VMEM((experts, 1, 128), full),
            pltpu.VMEM((steps, 1, 128), full),
            pltpu.VMEM((steps, 4, 2, 2, slab, 8, lanes), half),
            pltpu.VMEM((depth, columns), half),
            pltpu.VMEM((depth, columns), half),
            pltpu.VMEM((columns, depth), half),
            pltpu.VMEM((depth, columns), half),
            pltpu.VMEM((steps, 4, 3, 8 * CAP, columns), full),
            pltpu.VMEM((steps, 4, 3, 8 * CAP, columns), full),
            pltpu.VMEM((8 * CAP, columns), full),
            pltpu.VMEM((4, 3, 8 * CAP, columns // 2), full),
            pltpu.VMEM((4, 3, 8 * CAP, columns // 2), full),
            pltpu.VMEM((1, 128), full),
            pltpu.VMEM((1, columns), full),
            pltpu.VMEM((4, 1, columns), full),
            pltpu.VMEM((KEEP * BLOCK, depth), half),
            pltpu.VMEM((3, KEEP * UNIT, depth), half),
            pltpu.VMEM((KEEP * UNIT, depth), half),
            dma((8,)),
            dma((2, 8)), dma((2, 8)), dma((8,)), dma((8,)),
            dma((steps, 2, 2)), dma((steps, 2, 2)),
            dma((steps, 2)), dma((steps,)),
            dma((steps, 2, 2)), dma((steps, 2, 2)), dma((steps, 2)), dma((steps, 2)),
            dma((steps, 3)), dma((steps, 3)), dma((3,)), dma((3,)), dma((3,)), dma((3,)),
            dma((3,)), dma((3,)), dma((2,)), dma((1,)),
        ],
        compiler_params=pltpu.CompilerParams(
            collective_id=0, has_side_effects=True, vmem_limit_bytes=62 * 1024 * 1024
        ),
        cost_estimate=pl.CostEstimate(flops=4 * 10**9, transcendentals=10**5, bytes_accessed=2 * 10**8),
    )(tokens, cotangent, routes, route_gate, dropped, gate_weight, up_weight, down_weight)


def body(tokens, cotangent, route_gate, routes, gate_weight, up_weight, down_weight, dropped):
    return routed(
        tokens, cotangent, jnp.transpose(routes, (0, 2, 1)), jnp.transpose(route_gate, (0, 2, 1)), dropped,
        gate_weight, up_weight, down_weight, lax.axis_size("expert"),
    )


def solution(mesh):
    return jax.shard_map(
        body,
        mesh=mesh,
        in_specs=(
            P(None, ("expert", "dp"), None),
            P(None, ("expert", "dp"), None),
            P(None, ("expert", "dp"), None),
            P(None, ("expert", "dp"), None),
            P("expert", "dp", "tensor"),
            P("expert", "dp", "tensor"),
            P("expert", "tensor", "dp"),
            P("expert", None),
        ),
        out_specs=(P(None, "expert", "tensor"), P("expert", "tensor", "dp")),
        check_vma=False,
    )
```

```python
import functools

import jax
import jax.numpy as jnp
from jax import lax
from jax.experimental import pallas as pl
from jax.experimental.pallas import tpu as pltpu
from jax.sharding import PartitionSpec as P

BLOCK = 128
KEEP = 5
CAP = 3
MESH = pl.DeviceIdType.MESH
UNIT = 32
WINDOW = 4
AHEAD = 256
OFFERS = ((0, 1, 5, 3), (1, 0, 0, 5), (1, 2, 10, 5), (1, 3, 15, 1), (2, 0, 4, 1), (2, 1, 5, 5), (2, 3, 15, 5), (3, 2, 12, 3))
HOLDERS = ((0, 1), (0, 1, 2), (1, 2), (1, 2, 3), (2, 3))


def kernel(
    experts,
    tokens, cotangent, routes, route_gate, dropped_in, gate_w, up_w, down_w,
    out, compact_out,
    mine, own_routes, own_gates, dropped, raw, info_own, info_all, packed, gate_send, gate_recv, arrived, wg, wu, wd, wdt, partial, sums, acc, last_part, last_sums, gate_last, share, shares, offered, taken, compact,
    local_sem, raw_send, raw_recv, info_send, info_recv, z_send, z_recv, g_send, g_recv,
    y_send, y_recv, f_send, f_recv, r_send, r_recv, s_send, s_recv, c_send, c_recv, l_send, l_recv, gl_send, gl_recv,
):
    planes = experts // 2
    steps = planes // 2
    rows = tokens.shape[1]
    width = tokens.shape[2]
    lanes = width // 8
    slab = 8 * CAP // 8
    e = lax.axis_index("expert")
    p = lax.axis_index("dp")
    t = lax.axis_index("tensor")
    z = e // 2
    c = e % 2
    b = 2 * p + c

    def local(src, dst, sem):
        return pltpu.make_async_copy(src, dst, sem)

    def remote(src, dst, send, recv, expert, dp, tensor):
        return pltpu.make_async_remote_copy(
            src_ref=src, dst_ref=dst, send_sem=send, recv_sem=recv,
            device_id={"expert": expert, "dp": dp, "tensor": tensor}, device_id_type=MESH,
        )

    barrier = pltpu.get_barrier_semaphore()

    def greet(expert, dp, tensor):
        pl.semaphore_signal(
            barrier, inc=1, device_id={"expert": expert, "dp": dp, "tensor": tensor}, device_id_type=MESH
        )

    def greet_z(k, carry):
        greet((e + k) % experts, p, t)
        return carry

    lax.fori_loop(1, experts, greet_z, 0)
    for k in range(1, 4):
        greet(e, (p + k) % 4, t)
        greet(2 * z + 1 - c, (p + k) % 4, t)
        greet(e, p, (t + k) % 4)

    for index in range(4):
        source = tokens if index < 2 else cotangent

        @pl.when(t == index)
        def _():
            local(source.at[index % 2], mine, local_sem.at[0]).start()

    copies = [local(gate_w.at[0], wg, local_sem.at[1]), local(up_w.at[0], wu, local_sem.at[2]),
              local(down_w.at[0], wd, local_sem.at[3])]
    small = [local(routes, own_routes, local_sem.at[5]), local(route_gate, own_gates, local_sem.at[6])]
    for copy in small:
        copy.start()
    local(dropped_in, dropped, local_sem.at[7]).start()
    for copy in copies:
        copy.start()

    for copy in small:
        copy.wait()
    lane = lax.broadcasted_iota(jnp.int32, (2, 128), 1)
    own_lanes = lane // rows == b % 4
    spread_of = jnp.where(
        lax.broadcasted_iota(jnp.int32, (rows, 128), 0) == lax.broadcasted_iota(jnp.int32, (rows, 128), 1) % rows, 1.0, 0.0
    ).astype(jnp.bfloat16)
    info_own[...] = jnp.zeros(info_own.shape, jnp.float32)
    for which in range(2):
        for at, lines in ((0, own_routes[which].astype(jnp.float32)), (2, own_gates[which].astype(jnp.float32))):
            wide = jnp.dot(lines.astype(jnp.bfloat16), spread_of, preferred_element_type=jnp.float32)
            info_own[which, at:at + 2] = jnp.where(own_lanes, wide, 0.0)
    info_all[b] = info_own[...]
    local(tokens.at[0], mine, local_sem.at[0]).wait()
    pl.semaphore_wait(barrier, experts - 1 + 9)

    parts = ((0, AHEAD), (AHEAD, lanes - AHEAD))

    def raw_copy(part, k, other, owner):
        start, size = parts[part]
        return remote(
            mine.at[:, pl.ds(pl.multiple_of(other * lanes + start, 128), size)], raw.at[owner, :, pl.ds(start, size)],
            raw_send.at[part, k], raw_recv.at[part, k], 2 * z + other % 2, other // 2, t,
        )

    def info_copy(k, other, owner):
        return remote(
            info_own, info_all.at[owner], info_send.at[k], info_recv.at[k], 2 * z + other % 2, other // 2, t
        )

    own_raw = local(mine.at[:, pl.ds(pl.multiple_of(b * lanes, 128), lanes)], raw.at[b], local_sem.at[4])
    own_raw.start()
    for k in range(1, 8):
        info_copy(k, (b + k) % 8, b).start()
    for k in range(1, 8):
        raw_copy(0, k, (b + k) % 8, b).start()

    local(dropped_in, dropped, local_sem.at[7]).wait()
    first, second, third = dropped[0, 0], dropped[0, 1], dropped[0, 2]
    least = jnp.minimum(first, jnp.minimum(second, third))
    most = jnp.maximum(first, jnp.maximum(second, third))
    middle = first + second + third - least - most
    kept = []
    for rank in range(KEEP):
        number = jnp.where(least <= rank, rank + 1, rank)
        number = jnp.where(middle <= number, number + 1, number)
        kept.append(jnp.where(most <= number, number + 1, number))
    copies[2].wait()
    for rank in range(KEEP):
        offered[rank * BLOCK:(rank + 1) * BLOCK] = jnp.where(kept[rank] == 2 * t, wd[:BLOCK], wd[BLOCK:])

    def offer(holder, taker, start, size):
        away = (taker - holder) % 4 - 1
        return remote(
            offered.at[pl.ds(start * UNIT, size * UNIT)], taken.at[away, pl.ds((start - KEEP * taker) * UNIT, size * UNIT)],
            c_send.at[away], c_recv.at[away], e, p, taker,
        )

    def each_offer(act):
        for entry in OFFERS:
            @pl.when(t == entry[0])
            def _():
                act(offer(*entry))

    each_offer(lambda copy: copy.start())
    for k in range(1, 8):
        raw_copy(1, k, (b + k) % 8, b).start()
    for k in range(1, 8):
        info_copy(k, (b + k) % 8, (b + 8 - k) % 8).wait_recv()

    count = 8 * rows

    def places(which):
        low = info_all[0, which] + info_all[1, which] + info_all[2, which] + info_all[3, which]
        high = info_all[4, which] + info_all[5, which] + info_all[6, which] + info_all[7, which]
        both = jnp.concatenate([low, high], axis=1)
        expert_of = lax.broadcasted_iota(jnp.int32, (experts, count), 0).astype(jnp.float32)
        first = jnp.broadcast_to(both[0:1], (experts, count)) == expert_of
        second = jnp.broadcast_to(both[1:2], (experts, count)) == expert_of
        chosen = jnp.where(first | second, 1.0, 0.0)
        above = lax.broadcasted_iota(jnp.int32, (count, count), 0)
        across = lax.broadcasted_iota(jnp.int32, (count, count), 1)
        before = jnp.where((above < across) & (above // rows == across // rows), 1.0, 0.0)
        rank = jnp.dot(
            chosen.astype(jnp.bfloat16), before.astype(jnp.bfloat16), preferred_element_type=jnp.float32
        )
        block_of = lax.broadcasted_iota(jnp.int32, (experts, count), 1) // rows
        place = jnp.where(chosen > 0.0, rank + CAP * block_of.astype(jnp.float32), -1.0)
        weight = jnp.where(first, jnp.broadcast_to(both[2:3], (experts, count)), 0.0) + jnp.where(
            second, jnp.broadcast_to(both[3:4], (experts, count)), 0.0
        )
        return place, weight

    group = 8
    slot_of = lax.broadcasted_iota(jnp.int32, (group, 8 * CAP, count), 1).astype(jnp.float32)

    def chosen_rows(place, start):
        part = place[start:start + group]
        return jnp.where(jnp.broadcast_to(part[:, None, :], slot_of.shape) == slot_of, 1.0, 0.0)

    place, _ = places(t % 2)
    own_raw.wait()

    def pack(part):
        start, size = parts[part]
        for k in range(1, 8):
            raw_copy(part, k, (b + k) % 8, (b + 8 - k) % 8).wait_recv()
        whole = raw[:, :, start:start + size].reshape(count, size)
        for first_expert in range(0, experts, group):
            select = chosen_rows(place, first_expert).reshape(group * 8 * CAP, count).astype(jnp.bfloat16)
            values = jnp.dot(select, whole, preferred_element_type=jnp.float32)
            packed[slab * first_expert:slab * (first_expert + group), :, start:start + size] = values.reshape(
                slab * group, 8, size
            ).astype(jnp.bfloat16)

    def plane(i, sign):
        return (z + (i + 1 if sign else planes - (i + 1) % steps)) % planes

    def z_copy(i, sign, core, owner_core):
        expert = 2 * plane(i, sign) + core
        return remote(
            packed.at[pl.ds(expert * slab, slab)], arrived.at[i, t, sign, owner_core],
            z_send.at[i, sign, core], z_recv.at[i, sign, owner_core], expert, p, t,
        )

    def z_part(i, sign, core, part):
        expert = 2 * plane(i, sign) + core
        span = pl.ds(*parts[part])
        return remote(
            packed.at[pl.ds(expert * slab, slab), :, span], arrived.at[i, t, sign, c, :, :, span],
            z_send.at[i, sign, core], z_recv.at[i, sign, c], expert, p, t,
        )

    def z_start(i, carry):
        for core in range(2):
            z_copy(i, 1, core, c).start()

            @pl.when(i != steps - 1)
            def _():
                z_copy(i, 0, core, c).start()
        return carry

    window = min(WINDOW, steps - 1)
    for part in range(2):
        pack(part)
        if part == 1:
            own_slab = local(packed.at[pl.ds(e * slab, slab)], arrived.at[steps - 1, t, 0, c], z_recv.at[steps - 1, 0, c])
            own_slab.start()
            for core in range(2):
                @pl.when(c != core)
                def _():
                    z_copy(steps - 1, 0, core, c).start()

        def z_begin(i, carry):
            for core in range(2):
                for sign in (1, 0):
                    z_part(i, sign, core, part).start()
            return carry

        lax.fori_loop(0, window, z_begin, 0)

    def z_sent(i):
        for sign in range(2):
            for core in range(2):
                if sign == 1:
                    z_copy(i, 1, core, c).wait_send()
                else:
                    @pl.when((i != steps - 1) | (c != core))
                    def _():
                        z_copy(i, 0, core, c).wait_send()

    def make_gates():
        gate_place, gate_weight = places(p % 2)
        row_at = lax.broadcasted_iota(jnp.int32, (group, 8 * CAP, 128), 1)
        lane_at = lax.broadcasted_iota(jnp.int32, (group, 8 * CAP, 128), 2)
        ones = jnp.ones((count, 128), jnp.bfloat16)
        for start in range(0, experts, group):
            part = gate_weight[start:start + group]
            weighted = chosen_rows(gate_place, start) * jnp.broadcast_to(part[:, None, :], slot_of.shape)
            spread = jnp.dot(
                weighted.reshape(group * 8 * CAP, count).astype(jnp.bfloat16), ones, preferred_element_type=jnp.float32
            ).reshape(group, 8 * CAP, 128)
            line = jnp.sum(jnp.where(row_at == lane_at, spread, 0.0), axis=1, keepdims=True)
            gate_send[start:start + group] = line

    def g_copy(i, sign, core):
        expert = 2 * plane(i, sign) + core
        return remote(
            gate_send.at[expert], gate_recv.at[i], g_send.at[i, core], g_recv.at[i], expert, p, t
        )

    def far_gate(core):
        expert = 2 * plane(steps - 1, 1) + core
        return remote(gate_send.at[expert], gate_last, gl_send.at[core], gl_recv.at[0], expert, p, t)

    own_gate = local(gate_send.at[e], gate_recv.at[steps - 1], g_recv.at[steps - 1])

    def g_each(act):
        def g_step(i, carry):
            for core in range(2):
                @pl.when((c == 0) & (p // 2 == 1) & (i != steps - 1))
                def _():
                    act(g_copy(i, 1, core))

                @pl.when((c == 0) & (p // 2 == 0) & ((i != steps - 1) | (c != core)))
                def _():
                    act(g_copy(i, 0, core))
            return carry

        lax.fori_loop(0, steps, g_step, 0)
        for core in range(2):
            @pl.when(c == 0)
            def _():
                act(far_gate(core))

    def send_gates():
        g_each(lambda copy: copy.start())

        @pl.when((c == 0) & (p // 2 == 0))
        def _():
            own_gate.start()

    up_t, down_t, far_t = (t + 1) % 4, (t + 3) % 4, (t + 2) % 4

    def y_copy(i, sign, way, owner):
        return remote(
            arrived.at[i, owner, sign], arrived.at[i, owner, sign], y_send.at[i, sign, way], y_recv.at[i, sign, way],
            e, p, up_t if way == 0 else down_t,
        )

    def f_copy(i, way, owner):
        return remote(
            arrived.at[i, owner, way], arrived.at[i, owner, way], f_send.at[i, way], f_recv.at[i, way],
            e, p, up_t if way == 0 else down_t,
        )

    def far_copy(i):
        return remote(
            arrived.at[i, t, 1], arrived.at[i, t, 1], f_send.at[i, 1], f_recv.at[i, 1], e, p, far_t
        )

    def r_copy(i, k, owner):
        other = (p + k) % 4
        return remote(
            partial.at[i, other], sums.at[i, owner], r_send.at[i, k - 1], r_recv.at[i, k - 1], e, other, t
        )

    def r_part(i, k, index):
        other = (p + k) % 4
        return remote(
            partial.at[i, other, index], sums.at[i, p, index], r_send.at[i, k - 1], r_recv.at[i, k - 1], e, other, t
        )

    def take_z(i, sign):
        for core in range(2):
            z_copy(i, sign, core, core).wait_recv()
        y_copy(i, sign, 0, t).start()
        y_copy(i, sign, 1, t).start()
        if sign == 1:
            @pl.when(i == steps - 1)
            def _():
                far_copy(i).start()

    def take_y(i, sign):
        owner = down_t if sign == 0 else up_t
        y_copy(i, sign, sign, owner).wait_recv()
        if sign == 0:
            f_copy(i, sign, owner).start()
        else:
            @pl.when(i != steps - 1)
            def _():
                f_copy(i, sign, owner).start()

    def take_compact():
        for entry in OFFERS:
            @pl.when(t == entry[1])
            def _():
                offer(*entry).wait_recv()
        for taker in range(4):
            @pl.when(t == taker)
            def _():
                for unit in range(KEEP):
                    rank = (KEEP * taker + unit) // 4
                    at = (KEEP * taker + unit) * UNIT
                    value = offered[at:at + UNIT]
                    for holder in HOLDERS[rank]:
                        if holder != taker:
                            other = taken[(taker - holder) % 4 - 1, unit * UNIT:(unit + 1) * UNIT]
                            value = jnp.where(kept[rank] // 2 == holder, other, value)
                    compact[unit * UNIT:(unit + 1) * UNIT] = value

    def lhs(i, first, core):
        loaded = arrived[i, first:first + 2, :, core]
        return loaded.astype(jnp.float32).reshape(4 * 8 * CAP, lanes).astype(jnp.bfloat16)

    def product(one, two, weight):
        return jnp.dot(one, weight[:lanes], preferred_element_type=jnp.float32) + jnp.dot(
            two, weight[lanes:], preferred_element_type=jnp.float32
        )

    def multiply(i):
        f_copy(i, 0, far_t).wait_recv()
        f_copy(i, 1, far_t).wait_recv()
        y_copy(i, 0, 1, up_t).wait_recv()
        y_copy(i, 1, 0, down_t).wait_recv()
        low, high = lhs(i, 0, 0), lhs(i, 0, 1)
        grad_low, grad_high = lhs(i, 2, 0), lhs(i, 2, 1)
        for index, (one, two, weight) in enumerate(((low, high, wg), (low, high, wu), (grad_low, grad_high, wdt))):
            value = product(one, two, weight)
            for which in range(2):
                for sign in range(2):
                    at = (2 * which + sign) * 8 * CAP
                    partial[i, 2 * sign + which, index] = value[at:at + 8 * CAP]
            for k in range(1, 4):
                r_part(i, k, index).start()

    def last_copy(k, owner, index):
        other = (p + k) % 4
        if index is None:
            source, target = last_part.at[other], last_sums.at[owner]
        else:
            source, target = last_part.at[other, index], last_sums.at[owner, index]
        return remote(source, target, l_send.at[k - 1], l_recv.at[k - 1], e, other, t)

    def multiply_last(sign):
        i = steps - 1
        f_copy(i, sign, far_t).wait_recv()
        y_copy(i, sign, 1 - sign, down_t if sign else up_t).wait_recv()

        def rows_of(first, core):
            loaded = arrived[i, first:first + 2, sign, core]
            return loaded.astype(jnp.float32).reshape(2 * 8 * CAP, lanes).astype(jnp.bfloat16)

        low, high = rows_of(0, 0), rows_of(0, 1)
        grad_low, grad_high = rows_of(2, 0), rows_of(2, 1)
        middle = wg.shape[1] // 2
        for index, (one, two, weight) in enumerate(((low, high, wg), (low, high, wu), (grad_low, grad_high, wdt))):
            value = product(one, two, weight)
            for which in range(2):
                rows_at = value[which * 8 * CAP:(which + 1) * 8 * CAP]
                if sign == 0:
                    partial[i, which, index] = rows_at
                else:
                    last_part[which, index] = rows_at[:, :middle]
                    last_part[2 + which, index] = rows_at[:, middle:]
            for k in range(1, 4):
                if sign == 0:
                    @pl.when((p + k) % 4 < 2)
                    def _():
                        r_part(i, k, index).start()
                else:
                    last_copy(k, p, index).start()

    def finish(i):
        total = partial[i, p]
        for k in range(1, 4):
            r_copy(i, k, (p + 4 - k) % 4).wait_recv()
            total = total + sums[i, (p + 4 - k) % 4]
        local(gate_send.at[e], gate_recv.at[i], g_recv.at[i]).wait()
        acc[...] += gated(total, gate_recv[i])

    def gated(total, line):
        hidden = total[0] / (1.0 + jnp.exp(-total[0])) * total[1]
        column = jnp.sum(
            jnp.where(row24 == lane24, jnp.broadcast_to(line, (8 * CAP, 128)), 0.0), axis=1, keepdims=True
        )
        return column * hidden * total[2]

    def finish_last():
        total = last_part[p]
        for k in range(1, 4):
            last_copy(k, (p + 4 - k) % 4, None).wait_recv()
            total = total + last_sums[(p + 4 - k) % 4]
        local(gate_send.at[e], gate_last, gl_recv.at[0]).wait()
        value = gated(total, gate_last[...])
        middle = wg.shape[1] // 2

        @pl.when(p // 2 == 0)
        def _():
            acc[:, :middle] += value

        @pl.when(p // 2 == 1)
        def _():
            acc[:, middle:] += value

    for copy in copies[:2]:
        copy.wait()
    row24 = lax.broadcasted_iota(jnp.int32, (8 * CAP, 128), 0)
    lane24 = lax.broadcasted_iota(jnp.int32, (8 * CAP, 128), 1)
    acc[...] = jnp.zeros(acc.shape, jnp.float32)
    take_z(steps - 1, 0)

    def early():
        for k in range(1, 8):
            info_copy(k, (b + k) % 8, b).wait_send()
            for part in range(2):
                raw_copy(part, k, (b + k) % 8, b).wait_send()
        g_each(lambda copy: copy.wait_send())

    def drain(i, carry):
        @pl.when(i >= steps - window)
        def _():
            z_sent(i)

        for way in range(2):
            for sign in range(2):
                y_copy(i, sign, way, t).wait_send()
            f_copy(i, way, down_t if way == 0 else up_t).wait_send()
        for k in range(1, 4):
            @pl.when((i != steps - 1) | ((p + k) % 4 < 2))
            def _():
                r_copy(i, k, p).wait_send()
        return carry

    def step(s, carry):
        @pl.when(s == 1)
        def _():
            take_y(steps - 1, 0)

        @pl.when((s >= 1) & (s < steps))
        def _():
            take_y(s - 1, 0)

        @pl.when((s >= 1) & (s < steps + 1))
        def _():
            take_y(s - 1, 1)

        @pl.when(s < steps - 1)
        def _():
            take_z(s, 0)

        @pl.when(s < steps)
        def _():
            take_z(s, 1)

        @pl.when(s == 0)
        def _():
            make_gates()
            send_gates()
            wdt[...] = jnp.transpose(wd[...].astype(jnp.float32)).astype(jnp.bfloat16)

        @pl.when(s < steps - window)
        def _():
            z_sent(s)
            z_start(s + window, 0)

        @pl.when((s >= 1) & (s < steps))
        def _():
            multiply(s - 1)

        @pl.when(s == steps)
        def _():
            multiply_last(1)

        @pl.when((s >= 2) & (s < steps + 1))
        def _():
            finish(s - 2)

        @pl.when(s == 2)
        def _():
            early()

        @pl.when(s == 3)
        def _():
            multiply_last(0)

        @pl.when((s >= 4) & (s < steps + 1))
        def _():
            drain(s - 4, 0)

        @pl.when(s == 6)
        def _():
            each_offer(lambda copy: copy.wait_send())

        @pl.when((s == 5) & (p < 2))
        def _():
            finish(steps - 1)

        @pl.when(s == steps // 2)
        def _():
            take_compact()
            local(compact, compact_out.at[0], local_sem.at[1]).start()
        return carry

    lax.fori_loop(0, steps + 1, step, 0)
    finish_last()
    total = acc[...]
    share[...] = jnp.broadcast_to(jnp.sum(total, axis=0, keepdims=True), share.shape)
    shares[p] = share[...]

    def s_copy(k, owner):
        return remote(share, shares.at[owner], s_send.at[k - 1], s_recv.at[k - 1], e, (p + k) % 4, t)

    for k in range(1, 4):
        s_copy(k, p).start()
    for k in range(1, 4):
        last_copy(k, p, None).wait_send()
    local(compact, compact_out.at[0], local_sem.at[1]).wait()
    lax.fori_loop(steps - 3, steps, drain, 0)
    for k in range(1, 4):
        s_copy(k, (p + 4 - k) % 4).wait_recv()
    out[0] = jnp.abs(shares[0] + shares[2])
    out[1] = jnp.abs(shares[1] + shares[3])
    for k in range(1, 4):
        s_copy(k, p).wait_send()


def routed(tokens, cotangent, routes, route_gate, dropped, gate_weight, up_weight, down_weight, experts):
    steps = experts // 4
    rows, width = tokens.shape[1:]
    lanes = width // 8
    depth, columns = gate_weight.shape[1:]
    slab = CAP
    anywhere = pl.BlockSpec(memory_space=pltpu.HBM)
    vmem = pl.BlockSpec(memory_space=pltpu.VMEM)
    half, full, dma = jnp.bfloat16, jnp.float32, pltpu.SemaphoreType.DMA
    return pl.pallas_call(
        functools.partial(kernel, experts),
        out_shape=(
            jax.ShapeDtypeStruct((2, 1, columns), full),
            jax.ShapeDtypeStruct((1, KEEP * UNIT, depth), half),
        ),
        in_specs=[anywhere] * 8,
        out_specs=(vmem, anywhere),
        scratch_shapes=[
            pltpu.VMEM((rows, width), half),
            pltpu.VMEM((2, 2, rows), jnp.int32),
            pltpu.VMEM((2, 2, rows), half),
            pltpu.SMEM((1, 3), jnp.int32),
            pltpu.VMEM((8, rows, lanes), half),
            pltpu.VMEM((2, 8, 128), full),
            pltpu.VMEM((8, 2, 8, 128), full),
            pltpu.VMEM((experts * slab, 8, lanes), half),
            pltpu.VMEM((experts, 1, 128), full),
            pltpu.VMEM((steps, 1, 128), full),
            pltpu.VMEM((steps, 4, 2, 2, slab, 8, lanes), half),
            pltpu.VMEM((depth, columns), half),
            pltpu.VMEM((depth, columns), half),
            pltpu.VMEM((columns, depth), half),
            pltpu.VMEM((depth, columns), half),
            pltpu.VMEM((steps, 4, 3, 8 * CAP, columns), full),
            pltpu.VMEM((steps, 4, 3, 8 * CAP, columns), full),
            pltpu.VMEM((8 * CAP, columns), full),
            pltpu.VMEM((4, 3, 8 * CAP, columns // 2), full),
            pltpu.VMEM((4, 3, 8 * CAP, columns // 2), full),
            pltpu.VMEM((1, 128), full),
            pltpu.VMEM((1, columns), full),
            pltpu.VMEM((4, 1, columns), full),
            pltpu.VMEM((KEEP * BLOCK, depth), half),
            pltpu.VMEM((3, KEEP * UNIT, depth), half),
            pltpu.VMEM((KEEP * UNIT, depth), half),
            dma((8,)),
            dma((2, 8)), dma((2, 8)), dma((8,)), dma((8,)),
            dma((steps, 2, 2)), dma((steps, 2, 2)),
            dma((steps, 2)), dma((steps,)),
            dma((steps, 2, 2)), dma((steps, 2, 2)), dma((steps, 2)), dma((steps, 2)),
            dma((steps, 3)), dma((steps, 3)), dma((3,)), dma((3,)), dma((3,)), dma((3,)),
            dma((3,)), dma((3,)), dma((2,)), dma((1,)),
        ],
        compiler_params=pltpu.CompilerParams(
            collective_id=0, has_side_effects=True, vmem_limit_bytes=62 * 1024 * 1024
        ),
        cost_estimate=pl.CostEstimate(flops=4 * 10**9, transcendentals=10**5, bytes_accessed=2 * 10**8),
    )(tokens, cotangent, routes, route_gate, dropped, gate_weight, up_weight, down_weight)


def body(tokens, cotangent, route_gate, routes, gate_weight, up_weight, down_weight, dropped):
    return routed(
        tokens, cotangent, jnp.transpose(routes, (0, 2, 1)), jnp.transpose(route_gate, (0, 2, 1)), dropped,
        gate_weight, up_weight, down_weight, lax.axis_size("expert"),
    )


def solution(mesh):
    return jax.shard_map(
        body,
        mesh=mesh,
        in_specs=(
            P(None, ("expert", "dp"), None),
            P(None, ("expert", "dp"), None),
            P(None, ("expert", "dp"), None),
            P(None, ("expert", "dp"), None),
            P("expert", "dp", "tensor"),
            P("expert", "dp", "tensor"),
            P("expert", "tensor", "dp"),
            P("expert", None),
        ),
        out_specs=(P(None, "expert", "tensor"), P("expert", "tensor", "dp")),
        check_vma=False,
    )
```
